256 devices in a mesh: seq: 32 (over x, z), head: 8 (over y, core).
Axes of the slice: x: 4, y: 4, z: 8, core: 2. Of those that a mesh axis runs over, the one named last changes fastest.
Arguments:
- queries: bfloat16 [49152, 4096], P(('seq', 'head')), may hold values from -32 to 32
- cache_keys: bfloat16 [262144, 1024], P('seq', 'head'), may hold values from -12 to 12
- cache_values: bfloat16 [262144, 1024], P('seq', 'head'), may hold values from -6 to 6
- block_ids: int32 [384, 8], P('seq'), may hold values from 0 to 2047, as said below
Outputs:
- attention: bfloat16 [49152, 4096], P(('seq', 'head'))
The draws below stay inside these ranges and needn't reach their ends.
Inputs may be any that keep to these rules, and one draw needn't show every extreme that they name: `block_ids`: entries 0 to 4 of row r name distinct blocks c with c // 64 == r // 12; the other 3 entries name blocks with another value of c // 64, distinct within the row. Among the far entries of the 12 rows with one value of r // 12, at most 2 name blocks of any one other value of c // 64, and exactly 2 do for some value.
All inputs are finite; a program needn't handle non-finite values.
Results may differ from the reference program's by a relative error of at most 0.0043.
Values may be sent and summed in bfloat16 or wider, within the bound.
No kernel may reach another device: no remote copies, remote signals or barrier semaphores. Data moves between devices by JAX's collectives and lax.ppermute only.
A program may use at most 128 MiB of HBM per device.

```python
import jax
import jax.numpy as jnp
from jax import lax

QH = 32
KVH = 8
HD = 128
BLK = 128
PICKS = 8
NEAR = 5
QB_DEV = 12
KB_DEV = 64
FAR = 3
CAP = 2
QBLOCKS = 384
KBLOCKS = 2048
QTOK = 49152
KTOK = 262144
N_SEQ = 32


def draw_queries(key, part):
    row_count = QB_DEV * BLK * N_SEQ
    column_count = QH * HD
    drawn = jnp.clip(jax.random.normal(jax.random.fold_in(key, 1), (row_count, column_count), jnp.float32), -6.0, 6.0)
    return drawn.astype(jnp.bfloat16)


def draw_cache_keys(key, part):
    row_count = KB_DEV * BLK * N_SEQ
    column_count = KVH * HD
    drawn = jnp.clip(jax.random.normal(jax.random.fold_in(key, 2), (row_count, column_count), jnp.float32), -6.0, 6.0)
    return drawn.astype(jnp.bfloat16)


def draw_block_ids(key, part):

    def one_shard(shard_key, shard_index):
        near_keys = jax.random.split(jax.random.fold_in(shard_key, 1), QB_DEV)
        near_blocks = jax.vmap(lambda near_key: jax.random.permutation(near_key, KB_DEV))(near_keys)[:, :NEAR].astype(jnp.int32)
        others = N_SEQ - 1
        hot_owner = jax.random.randint(jax.random.fold_in(shard_key, 2), (), 0, others, dtype=jnp.int32)
        owner_pool = jnp.repeat(jnp.arange(others, dtype=jnp.int32), CAP)
        shuffle = jax.random.permutation(jax.random.fold_in(shard_key, 3), owner_pool.shape[0]).astype(jnp.int32)
        ordering = jnp.where(owner_pool == hot_owner, shuffle - owner_pool.shape[0], shuffle)
        chosen = owner_pool[jnp.argsort(ordering, stable=True)][:FAR * QB_DEV]
        chosen = chosen[jax.random.permutation(jax.random.fold_in(shard_key, 4), FAR * QB_DEV)]
        owner_of = (shard_index + 1 + chosen) % N_SEQ
        residue = jnp.arange(FAR, dtype=jnp.int32)[None, :]
        within = residue + FAR * jax.random.randint(jax.random.fold_in(shard_key, 5), (QB_DEV, FAR), 0, KB_DEV // FAR, dtype=jnp.int32)
        far_blocks = owner_of.reshape(QB_DEV, FAR) * KB_DEV + within
        return jnp.concatenate([shard_index * KB_DEV + near_blocks, far_blocks], axis=1)
    shard_keys = jax.random.split(key, N_SEQ)
    picked = jax.vmap(one_shard)(shard_keys, jnp.arange(N_SEQ, dtype=jnp.int32))
    return picked.reshape(N_SEQ * QB_DEV, PICKS).astype(jnp.int32)


def steps_of(stream_key, dims, shards, smallest, largest):
    gain, own = 1.0, jax.random.fold_in(stream_key, 6)
    for dim, shards_of in shards:
        heights = jnp.exp(jax.random.uniform(jax.random.fold_in(own, dim), (shards_of,), jnp.float32, smallest / len(shards), largest / len(shards)))
        gain = gain * jnp.repeat(heights, dims[dim] // shards_of).reshape([-1 if axis == dim else 1 for axis in range(len(dims))])
    return gain


def centred(rng, extent, deviation, bound, shards=(), kind=jnp.bfloat16):
    loudness = steps_of(rng, extent, shards, -0.22, 0.18) if shards else 1.0
    entries = jax.random.normal(rng, extent, jnp.float32) * deviation * loudness
    return jnp.minimum(jnp.maximum(entries, -bound), bound).astype(kind)


def setup_inputs(seed: int = 0) -> dict:
    key_list = jax.random.split(jax.random.key(seed), 5)
    queries = draw_queries(jax.random.fold_in(key_list[4], 71), 0)
    cache_keys = draw_cache_keys(jax.random.fold_in(key_list[4], 71), 0)
    cache_values = centred(key_list[2], (KTOK, KVH * HD), 1.0, 6.0, ((0, 32), (1, 8)))
    block_ids = draw_block_ids(jax.random.fold_in(key_list[4], 71), 0)
    return {"queries": queries, "cache_keys": cache_keys, "cache_values": cache_values, "block_ids": block_ids}


def block_partials(query_rows, key_rows, value_rows):
    score_scale = query_rows.shape[-1] ** -0.5
    scores = jnp.einsum("aqgrd,apkgd->apgrqk", query_rows.astype(jnp.float32), key_rows.astype(jnp.float32)) * score_scale
    block_max = jnp.max(scores, axis=-1)
    exponent = jnp.exp(scores - block_max[..., None])
    block_sum = jnp.sum(exponent, axis=-1)
    weight = lax.optimization_barrier(exponent.astype(jnp.bfloat16))
    partial_value = jnp.einsum("apgrqk,apkgd->apqgrd", weight.astype(jnp.float32), value_rows.astype(jnp.float32))
    return partial_value, block_max, block_sum


def merge_picks(partial_value, block_max, block_sum):
    highest = jnp.max(block_max, axis=-4, keepdims=True)
    factor = jnp.exp(block_max - highest)
    denominator = jnp.sum(factor * block_sum, axis=-4)
    numerator = jnp.sum(partial_value * jnp.moveaxis(factor, -1, -3)[..., None], axis=-5)
    return numerator / jnp.moveaxis(denominator, -1, -3)[..., None]


def reference(queries, cache_keys, cache_values, block_ids):
    ratio = QH // KVH
    query_blocks = queries.reshape(QBLOCKS, BLK, KVH, ratio, HD)
    key_blocks = cache_keys.reshape(KBLOCKS, BLK, KVH, HD)
    value_blocks = cache_values.reshape(KBLOCKS, BLK, KVH, HD)

    def attend_block(pieces):
        query_block, picked = pieces
        chosen_keys = jnp.take(key_blocks, picked.astype(jnp.int32), axis=0)
        chosen_values = jnp.take(value_blocks, picked.astype(jnp.int32), axis=0)
        partial_value, block_max, block_sum = block_partials(query_block[None], chosen_keys[None], chosen_values[None])
        return merge_picks(partial_value, block_max, block_sum)[0].astype(jnp.bfloat16)

    combined = lax.map(attend_block, (query_blocks, block_ids))
    return combined.reshape(QTOK, QH * HD)
```

```python
import functools
import math

import jax
import jax.numpy as jnp
from jax import lax
from jax.experimental import pallas as pl
from jax.experimental.pallas import tpu as pltpu
from jax.sharding import PartitionSpec as P

HD = 128
BLK = 128
NEAR = 5
CORES = 2
HBM = pl.BlockSpec(memory_space=pltpu.HBM)
SMEM = pl.BlockSpec(memory_space=pltpu.SMEM)
VMEM = pl.BlockSpec(memory_space=pltpu.VMEM)
LOG2E = 1.4426950408889634


def wait_for(ref, sem):
    pltpu.make_async_copy(ref, ref, sem).wait()


def cost(flops, bytes_accessed, transcendentals=0):
    return pl.CostEstimate(flops=flops, bytes_accessed=bytes_accessed, transcendentals=transcendentals)


def split_queries_kernel(offsets, places_ref, q_ref, *refs):
    outs, sem = refs[:-1], refs[-1]
    width = outs[0].shape[1]
    copies = []
    for i in range(offsets):
        start = pl.multiple_of(places_ref[i] * width, width)
        copies.append(pltpu.make_async_copy(q_ref.at[:, pl.ds(start, width)], outs[i], sem.at[i]))
    for copy in copies:
        copy.start()
    for copy in copies:
        copy.wait()


def split_queries(queries, places):
    count = places.shape[0]
    rows, width = queries.shape[0], queries.shape[1] // count
    return pl.pallas_call(
        functools.partial(split_queries_kernel, count),
        out_shape=[jax.ShapeDtypeStruct((rows, width), queries.dtype)] * count,
        in_specs=[SMEM, HBM],
        out_specs=[HBM] * count,
        scratch_shapes=[pltpu.SemaphoreType.DMA((count,))],
        cost_estimate=cost(0, 4 * queries.size),
    )(places, queries)


def join_outputs_kernel(offsets, places_ref, *refs):
    pieces, out_ref, sem = refs[:offsets], refs[offsets], refs[offsets + 1]
    width = pieces[0].shape[1]
    copies = []
    for i in range(offsets):
        start = pl.multiple_of(places_ref[i] * width, width)
        copies.append(pltpu.make_async_copy(pieces[i], out_ref.at[:, pl.ds(start, width)], sem.at[i]))
    for copy in copies:
        copy.start()
    for copy in copies:
        copy.wait()


def join_outputs(pieces, places):
    count = len(pieces)
    rows, width = pieces[0].shape
    return pl.pallas_call(
        functools.partial(join_outputs_kernel, count),
        out_shape=jax.ShapeDtypeStruct((rows, width * count), pieces[0].dtype),
        in_specs=[SMEM] + [HBM] * count,
        out_specs=HBM,
        scratch_shapes=[pltpu.SemaphoreType.DMA((count,))],
        cost_estimate=cost(0, 4 * rows * width * count),
    )(places, *pieces)


def pack_kernel(wanted_ref, k_ref, v_ref, out_ref, sem):
    count = out_ref.shape[0]

    def start(i, carry):
        rows = pl.ds(pl.multiple_of(wanted_ref[i] * BLK, BLK), BLK)
        pltpu.make_async_copy(k_ref.at[rows], out_ref.at[i, 0], sem).start()
        pltpu.make_async_copy(v_ref.at[rows], out_ref.at[i, 1], sem).start()
        return carry

    lax.fori_loop(0, count, start, 0)
    wait_for(out_ref, sem)


def pack(wanted, keys, values):
    count = wanted.shape[0]
    return pl.pallas_call(
        pack_kernel,
        out_shape=jax.ShapeDtypeStruct((count, 2, BLK, HD), keys.dtype),
        in_specs=[SMEM, HBM, HBM],
        out_specs=HBM,
        scratch_shapes=[pltpu.SemaphoreType.DMA],
        cost_estimate=cost(0, 8 * count * BLK * HD),
    )(wanted, keys, values)


def load_queries(core, qa_ref, qb_ref, q_buf, q_sem):
    half = qa_ref.shape[0]
    copies = []
    for i, (ref, place) in enumerate(((qa_ref, core), (qb_ref, 1 - core))):
        rows = pl.ds(pl.multiple_of(place * half, half), half)
        copies.append(pltpu.make_async_copy(ref, q_buf.at[rows], q_sem.at[i]))
    return copies


def near_kernel(ids_ref, core_ref, qa_ref, qb_ref, k_ref, v_ref, acc_ref, stat_ref, q_buf, k_buf, v_buf, q_sem, k_sem, v_sem):
    blocks, span = k_buf.shape[0], k_buf.shape[1]
    picks, ratio = span // BLK, q_buf.shape[1] // HD
    factor = HD ** (-0.5) * LOG2E
    q_copies = load_queries(core_ref[0], qa_ref, qb_ref, q_buf, q_sem)
    for copy in q_copies:
        copy.start()
    for i in range(blocks):
        for j in range(picks):
            rows = pl.ds(pl.multiple_of(ids_ref[i * picks + j] * BLK, BLK), BLK)
            pltpu.make_async_copy(k_ref.at[rows], k_buf.at[i, pl.ds(j * BLK, BLK)], k_sem.at[i]).start()
            pltpu.make_async_copy(v_ref.at[rows], v_buf.at[i, pl.ds(j * BLK, BLK)], v_sem.at[i]).start()
    for copy in q_copies:
        copy.wait()

    def block(i, carry):
        wait_for(k_buf.at[i], k_sem.at[i])
        wait_for(v_buf.at[i], v_sem.at[i])
        rows = pl.ds(pl.multiple_of(i * BLK, BLK), BLK)
        lane = lax.broadcasted_iota(jnp.int32, (BLK, HD), 1)
        stats = jnp.zeros((BLK, HD), jnp.float32)
        for r in range(ratio):
            columns = pl.ds(r * HD, HD)
            score = lax.dot_general(
                q_buf[rows, columns], k_buf[i], (((1,), (1,)), ((), ())), preferred_element_type=jnp.float32
            )
            highest = jnp.max(score, axis=1, keepdims=True) * factor
            exponent = jnp.exp2(score * factor - highest)
            total = jnp.sum(exponent, axis=1, keepdims=True)
            acc_ref[rows, columns] = jnp.dot(
                exponent.astype(jnp.bfloat16), v_buf[i], preferred_element_type=jnp.float32
            )
            stats = jnp.where(lane == r, highest, stats)
            stats = jnp.where(lane == ratio + r, total, stats)
        stat_ref[rows, :] = stats
        return carry

    lax.fori_loop(0, blocks, block, 0)


def near_attention(ids, core, qa, qb, keys, values):
    blocks, picks = ids.shape
    rows, width = 2 * qa.shape[0], qa.shape[1]
    span = picks * BLK
    work = rows * width * span
    return pl.pallas_call(
        near_kernel,
        out_shape=[
            jax.ShapeDtypeStruct((rows, width), jnp.float32),
            jax.ShapeDtypeStruct((rows, HD), jnp.float32),
        ],
        in_specs=[SMEM, SMEM, HBM, HBM, HBM, HBM],
        out_specs=[VMEM, VMEM],
        scratch_shapes=[
            pltpu.VMEM((rows, width), qa.dtype),
            pltpu.VMEM((blocks, span, HD), keys.dtype),
            pltpu.VMEM((blocks, span, HD), keys.dtype),
            pltpu.SemaphoreType.DMA((2,)),
            pltpu.SemaphoreType.DMA((blocks,)),
            pltpu.SemaphoreType.DMA((blocks,)),
        ],
        cost_estimate=cost(4 * work, 6 * rows * width + 4 * blocks * span * HD, work // HD),
    )(ids.reshape(-1), core, qa, qb, keys, values)


def far_kernel(slots_ref, core_ref, qa_ref, qb_ref, got_ref, acc_ref, stat_ref, oa_ref, ob_ref, q_buf, k_buf, v_buf, o_buf, q_sem, k_sem, v_sem, o_sem):
    blocks, span = k_buf.shape[0], k_buf.shape[1]
    picks, ratio = span // BLK, q_buf.shape[1] // HD
    half = qa_ref.shape[0]
    factor = HD ** (-0.5) * LOG2E
    core = core_ref[0]
    q_copies = load_queries(core, qa_ref, qb_ref, q_buf, q_sem)
    for copy in q_copies:
        copy.start()
    for i in range(blocks):
        for j in range(picks):
            slot = slots_ref[i * picks + j]
            pltpu.make_async_copy(got_ref.at[slot, 0], k_buf.at[i, pl.ds(j * BLK, BLK)], k_sem.at[i]).start()
            pltpu.make_async_copy(got_ref.at[slot, 1], v_buf.at[i, pl.ds(j * BLK, BLK)], v_sem.at[i]).start()
    for copy in q_copies:
        copy.wait()

    def block(i, carry):
        wait_for(k_buf.at[i], k_sem.at[i])
        wait_for(v_buf.at[i], v_sem.at[i])
        rows = pl.ds(pl.multiple_of(i * BLK, BLK), BLK)
        for r in range(ratio):
            columns = pl.ds(r * HD, HD)
            score = lax.dot_general(
                q_buf[rows, columns], k_buf[i], (((1,), (1,)), ((), ())), preferred_element_type=jnp.float32
            )
            before = stat_ref[rows, r : r + 1]
            highest = jnp.maximum(jnp.max(score, axis=1, keepdims=True) * factor, before)
            exponent = jnp.exp2(score * factor - highest)
            kept = jnp.exp2(before - highest)
            total = jnp.sum(exponent, axis=1, keepdims=True) + kept * stat_ref[rows, ratio + r : ratio + r + 1]
            partial = jnp.dot(exponent.astype(jnp.bfloat16), v_buf[i], preferred_element_type=jnp.float32)
            merged = (partial + kept * acc_ref[rows, columns]) / total
            o_buf[rows, columns] = merged.astype(o_buf.dtype)
        return carry

    lax.fori_loop(0, blocks, block, 0)
    copies = []
    for i, (ref, place) in enumerate(((oa_ref, core), (ob_ref, 1 - core))):
        rows = pl.ds(pl.multiple_of(place * half, half), half)
        copies.append(pltpu.make_async_copy(o_buf.at[rows], ref, o_sem.at[i]))
    for copy in copies:
        copy.start()
    for copy in copies:
        copy.wait()


def far_attention(slots, core, qa, qb, got, acc, stats):
    blocks, picks = slots.shape
    half, width = qa.shape
    rows = 2 * half
    span = picks * BLK
    work = rows * width * span
    return pl.pallas_call(
        far_kernel,
        out_shape=[jax.ShapeDtypeStruct((half, width), qa.dtype)] * 2,
        in_specs=[SMEM, SMEM, HBM, HBM, HBM, VMEM, VMEM],
        out_specs=[HBM, HBM],
        scratch_shapes=[
            pltpu.VMEM((rows, width), qa.dtype),
            pltpu.VMEM((blocks, span, HD), got.dtype),
            pltpu.VMEM((blocks, span, HD), got.dtype),
            pltpu.VMEM((rows, width), qa.dtype),
            pltpu.SemaphoreType.DMA((2,)),
            pltpu.SemaphoreType.DMA((blocks,)),
            pltpu.SemaphoreType.DMA((blocks,)),
            pltpu.SemaphoreType.DMA((2,)),
        ],
        cost_estimate=cost(4 * work, 8 * rows * width + 4 * blocks * span * HD, work // HD),
    )(slots.reshape(-1), core, qa, qb, got, acc, stats)


def offset_pairs(chips, chip_step, core_step):
    return [
        (chip * CORES + core, (chip + chip_step) % chips * CORES + (core ^ core_step))
        for chip in range(chips)
        for core in range(CORES)
    ]


def shards(queries, cache_keys, cache_values, block_ids):
    seq_count = lax.axis_size("seq")
    heads = lax.axis_size("head")
    seq_place = lax.axis_index("seq")
    head_place = lax.axis_index("head")
    chips = heads // CORES
    chip, core = head_place // CORES, head_place % CORES
    q_count, k_count = block_ids.shape[0], cache_keys.shape[0] // BLK
    per_chip = q_count // chips
    far_count = block_ids.shape[1] - NEAR
    capacity = max(2, (far_count * q_count + seq_count - 2) // (seq_count - 1))
    slot_total = seq_count * capacity

    far_ids = block_ids[:, NEAR:].reshape(-1)
    far_owner = far_ids // k_count
    far_within = far_ids - far_owner * k_count
    entry = jnp.arange(far_ids.shape[0], dtype=jnp.int32)
    earlier = (far_owner[:, None] == far_owner[None, :]) & (entry[None, :] < entry[:, None])
    far_slot = far_owner * capacity + jnp.sum(earlier.astype(jnp.int32), axis=1)
    placed = far_slot[:, None] == jnp.arange(slot_total, dtype=jnp.int32)[None, :]
    asked = jnp.sum(jnp.where(placed, far_within[:, None], 0), axis=0).reshape(seq_count, capacity)
    wanted = lax.all_to_all(asked, "seq", split_axis=0, concat_axis=0, tiled=True).reshape(-1)

    sent = pack(wanted, cache_keys, cache_values)
    got = lax.all_to_all(
        sent.reshape(seq_count, capacity, 2, BLK, HD), "seq", split_axis=0, concat_axis=0, tiled=True
    ).reshape(slot_total, 2, BLK, HD)

    steps = [(d, e) for d in range(chips) for e in range(CORES)]
    step_chip = jnp.array([d for d, _ in steps], jnp.int32)
    step_core = jnp.array([e for _, e in steps], jnp.int32)
    ahead = (chip + step_chip) % chips * CORES + (core + step_core) % CORES
    pieces = split_queries(queries, ahead)
    rows_of = {}
    for piece, (d, e) in zip(pieces, steps):
        rows_of[d, e] = piece if d == e == 0 else lax.ppermute(piece, "head", offset_pairs(chips, d, e))

    order = (chip - jnp.arange(chips, dtype=jnp.int32)) % chips
    near_ids = jnp.take((block_ids[:, :NEAR] - seq_place * k_count).reshape(chips, per_chip, NEAR), order, axis=0)
    slots = jnp.take(far_slot.reshape(chips, per_chip, far_count), order, axis=0)
    core_operand = core.astype(jnp.int32).reshape(1)

    near = [
        near_attention(near_ids[d], core_operand, rows_of[d, 0], rows_of[d, 1], cache_keys, cache_values)
        for d in range(chips)
    ]
    got, near = lax.optimization_barrier((got, near))
    results = {}
    for d in sorted(range(chips), key=lambda d: -min(d, chips - d)):
        made = far_attention(slots[d], core_operand, rows_of[d, 0], rows_of[d, 1], got, *near[d])
        for e in range(CORES):
            results[d, e] = made[e] if d == e == 0 else lax.ppermute(made[e], "head", offset_pairs(chips, -d, e))
    return join_outputs([results[step] for step in steps], ahead)


def solution(mesh):
    return jax.shard_map(
        shards,
        mesh=mesh,
        in_specs=(P(("seq", "head"), None), P("seq", "head"), P("seq", "head"), P("seq", None)),
        out_specs=P(("seq", "head"), None),
        check_vma=False,
    )
```

```python
import functools
import math

import jax
import jax.numpy as jnp
from jax import lax
from jax.experimental import pallas as pl
from jax.experimental.pallas import tpu as pltpu
from jax.sharding import PartitionSpec as P

HD = 128
BLK = 128
NEAR = 5
CORES = 2
HBM = pl.BlockSpec(memory_space=pltpu.HBM)
SMEM = pl.BlockSpec(memory_space=pltpu.SMEM)
VMEM = pl.BlockSpec(memory_space=pltpu.VMEM)
LOG2E = 1.4426950408889634


def wait_for(ref, sem):
    pltpu.make_async_copy(ref, ref, sem).wait()


def room(mebibytes):
    return pltpu.CompilerParams(vmem_limit_bytes=mebibytes * 1024 * 1024)


def cost(flops, bytes_accessed, transcendentals=0):
    return pl.CostEstimate(flops=flops, bytes_accessed=bytes_accessed, transcendentals=transcendentals)


def split_queries_kernel(places_ref, q_ref, *refs):
    count = len(refs) - 3
    outs, buf, in_sem, out_sem = refs[:count], *refs[count:]
    width = buf.shape[2]
    into, out_of = [], []
    for i in range(count):
        start = pl.multiple_of(places_ref[i] * width, width)
        into.append(pltpu.make_async_copy(q_ref.at[:, pl.ds(start, width)], buf.at[i], in_sem.at[i]))
        out_of.append(pltpu.make_async_copy(buf.at[i], outs[i], out_sem.at[i]))
    for copy in into:
        copy.start()
    for i in range(count):
        into[i].wait()
        out_of[i].start()
    for copy in out_of:
        copy.wait()


def split_queries(queries, places):
    count = places.shape[0]
    rows, width = queries.shape[0], queries.shape[1] // count
    return pl.pallas_call(
        split_queries_kernel,
        out_shape=[jax.ShapeDtypeStruct((rows, width), queries.dtype)] * count,
        in_specs=[SMEM, HBM],
        out_specs=[HBM] * count,
        scratch_shapes=[
            pltpu.VMEM((count, rows, width), queries.dtype),
            pltpu.SemaphoreType.DMA((count,)),
            pltpu.SemaphoreType.DMA((count,)),
        ],
        cost_estimate=cost(0, 4 * queries.size),
    )(places, queries)


def join_outputs_kernel(offsets, places_ref, *refs):
    pieces, out_ref, sem = refs[:offsets], refs[offsets], refs[offsets + 1]
    width = pieces[0].shape[1]
    copies = []
    for i in range(offsets):
        start = pl.multiple_of(places_ref[i] * width, width)
        copies.append(pltpu.make_async_copy(pieces[i], out_ref.at[:, pl.ds(start, width)], sem.at[i]))
    for copy in copies:
        copy.start()
    for copy in copies:
        copy.wait()


def join_outputs(pieces, places):
    count = len(pieces)
    rows, width = pieces[0].shape
    return pl.pallas_call(
        functools.partial(join_outputs_kernel, count),
        out_shape=jax.ShapeDtypeStruct((rows, width * count), pieces[0].dtype),
        in_specs=[SMEM] + [VMEM] * count,
        out_specs=HBM,
        scratch_shapes=[pltpu.SemaphoreType.DMA((count,))],
        compiler_params=room(4),
        cost_estimate=cost(0, 4 * rows * width * count),
    )(places, *pieces)


def pack_kernel(chunks, wanted_ref, k_ref, v_ref, out_ref, buf, in_sem, out_sem):
    span = out_ref.shape[0] // chunks
    for chunk in range(chunks):

        def start(i, carry):
            rows = pl.ds(pl.multiple_of(wanted_ref[i] * BLK, BLK), BLK)
            pltpu.make_async_copy(k_ref.at[rows], buf.at[i, 0], in_sem.at[chunk]).start()
            pltpu.make_async_copy(v_ref.at[rows], buf.at[i, 1], in_sem.at[chunk]).start()
            return carry

        lax.fori_loop(chunk * span, (chunk + 1) * span, start, 0, unroll=True)
    copies = []
    for chunk in range(chunks):
        part = pl.ds(chunk * span, span)
        wait_for(buf.at[part], in_sem.at[chunk])
        copies.append(pltpu.make_async_copy(buf.at[part], out_ref.at[part], out_sem.at[chunk]))
        copies[-1].start()
    for copy in copies:
        copy.wait()


def pack(wanted, keys, values):
    count, chunks = wanted.shape[0], 4
    return pl.pallas_call(
        functools.partial(pack_kernel, chunks),
        out_shape=jax.ShapeDtypeStruct((count, 2, BLK, HD), keys.dtype),
        in_specs=[SMEM, HBM, HBM],
        out_specs=HBM,
        scratch_shapes=[
            pltpu.VMEM((count, 2, BLK, HD), keys.dtype),
            pltpu.SemaphoreType.DMA((chunks,)),
            pltpu.SemaphoreType.DMA((chunks,)),
        ],
        cost_estimate=cost(0, 8 * count * BLK * HD),
    )(wanted, keys, values)


def scores_of(keys, queries):
    return lax.dot_general(keys, queries, (((1,), (1,)), ((), ())), preferred_element_type=jnp.float32)


def weighted(values, weights):
    return lax.dot_general(values, weights, (((0,), (0,)), ((), ())), preferred_element_type=jnp.float32)


def near_kernel(ids_ref, core_ref, qa_ref, qb_ref, k_ref, v_ref, acc_out, stat_out, q_out, q_buf, k_buf, v_buf, acc_ref, stat_ref, q_ref, k_sem, v_sem, out_sem):
    blocks, picks, half = acc_ref.shape[0], k_buf.shape[1] // BLK, qa_ref.shape[0]
    ratio = q_buf.shape[1] // HD
    factor = HD ** (-0.5) * LOG2E
    core = core_ref[0]
    for i in range(blocks):
        for j in range(picks):
            held = pl.ds(pl.multiple_of(ids_ref[i * picks + j] * BLK, BLK), BLK)
            pltpu.make_async_copy(k_ref.at[held], k_buf.at[i, pl.ds(j * BLK, BLK)], k_sem.at[i]).start()
            pltpu.make_async_copy(v_ref.at[held], v_buf.at[i, pl.ds(j * BLK, BLK)], v_sem.at[i]).start()
    q_buf[pl.ds(pl.multiple_of(core * half, half), half), :] = qa_ref[...]
    q_buf[pl.ds(pl.multiple_of((1 - core) * half, half), half), :] = qb_ref[...]
    for i in range(blocks):
        for r in range(ratio):
            q_ref[i, r * BLK : (r + 1) * BLK, :] = q_buf[i * BLK : (i + 1) * BLK, r * HD : (r + 1) * HD]
    copies = [pltpu.make_async_copy(q_ref, q_out, out_sem.at[0])]
    copies[0].start()

    def block(i, carry):
        wait_for(k_buf.at[i], k_sem.at[i])
        wait_for(v_buf.at[i], v_sem.at[i])
        score = scores_of(k_buf[i], q_ref[i])
        highest = jnp.max(score, axis=0, keepdims=True) * factor
        exponent = jnp.exp2(score * factor - highest)
        stat_ref[i, 0:1, :] = highest
        stat_ref[i, 1:2, :] = jnp.sum(exponent, axis=0, keepdims=True)
        acc_ref[i] = weighted(v_buf[i], exponent.astype(jnp.bfloat16))
        return carry

    lax.fori_loop(0, blocks, block, 0)
    copies.append(pltpu.make_async_copy(acc_ref, acc_out, out_sem.at[1]))
    copies.append(pltpu.make_async_copy(stat_ref, stat_out, out_sem.at[2]))
    copies[1].start()
    copies[2].start()
    for copy in copies:
        copy.wait()


def near_attention(ids, core, qa, qb, keys, values):
    blocks, picks = ids.shape
    rows, width = 2 * qa.shape[0], qa.shape[1]
    span, wide = picks * BLK, BLK * (width // HD)
    work = rows * width * span
    kept = [((blocks, HD, wide), jnp.float32), ((blocks, 8, wide), jnp.float32), ((blocks, wide, HD), qa.dtype)]
    return pl.pallas_call(
        near_kernel,
        out_shape=[jax.ShapeDtypeStruct(*what) for what in kept],
        in_specs=[SMEM, SMEM, VMEM, VMEM, HBM, HBM],
        out_specs=[HBM] * 3,
        scratch_shapes=[
            pltpu.VMEM((rows, width), qa.dtype),
            pltpu.VMEM((blocks, span, HD), keys.dtype),
            pltpu.VMEM((blocks, span, HD), keys.dtype),
            *[pltpu.VMEM(*what) for what in kept],
            pltpu.SemaphoreType.DMA((blocks,)),
            pltpu.SemaphoreType.DMA((blocks,)),
            pltpu.SemaphoreType.DMA((3,)),
        ],
        cost_estimate=cost(4 * work, 8 * rows * width + 4 * blocks * span * HD, work // HD),
    )(ids.reshape(-1), core, qa, qb, keys, values)


def far_kernel(slots_ref, core_ref, got_ref, acc_in, stat_in, q_in, oa_ref, ob_ref, k_buf, v_buf, acc_ref, stat_ref, q_ref, o_buf, k_sem, v_sem, in_sem, out_sem):
    blocks, picks = k_buf.shape[0], k_buf.shape[1] // BLK
    half, ratio = oa_ref.shape[0], oa_ref.shape[1] // HD
    factor = HD ** (-0.5) * LOG2E
    core = core_ref[0]
    kept_copies = []
    for i in range(blocks):
        copy = pltpu.make_async_copy(q_in.at[i], q_ref.at[i], in_sem.at[i, 0])
        copy.start()
        for j in range(picks):
            slot = slots_ref[i * picks + j]
            pltpu.make_async_copy(got_ref.at[slot, 0], k_buf.at[i, pl.ds(j * BLK, BLK)], k_sem.at[i]).start()
            pltpu.make_async_copy(got_ref.at[slot, 1], v_buf.at[i, pl.ds(j * BLK, BLK)], v_sem.at[i]).start()
        stat_copy = pltpu.make_async_copy(stat_in.at[i], stat_ref.at[i], in_sem.at[i, 1])
        acc_copy = pltpu.make_async_copy(acc_in.at[i], acc_ref.at[i], in_sem.at[i, 2])
        stat_copy.start()
        acc_copy.start()
        kept_copies.append((copy, stat_copy, acc_copy))
    for i in range(blocks):
        wait_for(k_buf.at[i], k_sem.at[i])
        wait_for(v_buf.at[i], v_sem.at[i])
        for copy in kept_copies[i]:
            copy.wait()
        score = scores_of(k_buf[i], q_ref[i])
        before = stat_ref[i, 0:1, :]
        highest = jnp.maximum(jnp.max(score, axis=0, keepdims=True) * factor, before)
        exponent = jnp.exp2(score * factor - highest)
        kept = jnp.exp2(before - highest)
        total = jnp.sum(exponent, axis=0, keepdims=True) + kept * stat_ref[i, 1:2, :]
        partial = weighted(v_buf[i], exponent.astype(jnp.bfloat16))
        merged = (partial + kept * acc_ref[i]) * (1.0 / total)
        for r in range(ratio):
            columns = slice(r * BLK, (r + 1) * BLK)
            o_buf[i * BLK : (i + 1) * BLK, columns] = merged[:, columns].T.astype(o_buf.dtype)
    copies = []
    for i, (ref, place) in enumerate(((oa_ref, core), (ob_ref, 1 - core))):
        rows = pl.ds(pl.multiple_of(place * half, half), half)
        copies.append(pltpu.make_async_copy(o_buf.at[rows], ref, out_sem.at[i]))
    for copy in copies:
        copy.start()
    for copy in copies:
        copy.wait()


def far_attention(slots, core, got, acc, stats, q):
    blocks, picks = slots.shape
    rows, width = blocks * BLK, q.shape[1] // BLK * HD
    span = picks * BLK
    work = rows * width * span
    return pl.pallas_call(
        far_kernel,
        out_shape=[jax.ShapeDtypeStruct((rows // 2, width), q.dtype)] * 2,
        in_specs=[SMEM, SMEM, HBM, HBM, HBM, HBM],
        out_specs=[HBM, HBM],
        scratch_shapes=[
            pltpu.VMEM((blocks, span, HD), got.dtype),
            pltpu.VMEM((blocks, span, HD), got.dtype),
            pltpu.VMEM(acc.shape, acc.dtype),
            pltpu.VMEM(stats.shape, stats.dtype),
            pltpu.VMEM(q.shape, q.dtype),
            pltpu.VMEM((rows, width), q.dtype),
            pltpu.SemaphoreType.DMA((blocks,)),
            pltpu.SemaphoreType.DMA((blocks,)),
            pltpu.SemaphoreType.DMA((blocks, 3)),
            pltpu.SemaphoreType.DMA((2,)),
        ],
        cost_estimate=cost(4 * work, 8 * rows * width + 4 * blocks * span * HD, work // HD),
    )(slots.reshape(-1), core, got, acc, stats, q)


def offset_pairs(chips, chip_step, core_step):
    return [
        (chip * CORES + core, (chip + chip_step) % chips * CORES + (core ^ core_step))
        for chip in range(chips)
        for core in range(CORES)
    ]


def shards(queries, cache_keys, cache_values, block_ids):
    seq_count = lax.axis_size("seq")
    heads = lax.axis_size("head")
    seq_place = lax.axis_index("seq")
    head_place = lax.axis_index("head")
    chips = heads // CORES
    chip, core = head_place // CORES, head_place % CORES
    q_count, k_count = block_ids.shape[0], cache_keys.shape[0] // BLK
    per_chip = q_count // chips
    far_count = block_ids.shape[1] - NEAR
    capacity = max(2, (far_count * q_count + seq_count - 2) // (seq_count - 1))
    slot_total = seq_count * capacity

    far_ids = block_ids[:, NEAR:].reshape(-1)
    far_owner = far_ids // k_count
    far_within = far_ids - far_owner * k_count
    entry = jnp.arange(far_ids.shape[0], dtype=jnp.int32)
    earlier = (far_owner[:, None] == far_owner[None, :]) & (entry[None, :] < entry[:, None])
    far_slot = far_owner * capacity + jnp.sum(earlier.astype(jnp.int32), axis=1)
    placed = far_slot[:, None] == jnp.arange(slot_total, dtype=jnp.int32)[None, :]
    asked = jnp.sum(jnp.where(placed, far_within[:, None], 0), axis=0).reshape(seq_count, capacity)
    wanted = lax.all_to_all(asked, "seq", split_axis=0, concat_axis=0, tiled=True).reshape(-1)

    sent = pack(wanted, cache_keys, cache_values)
    got = lax.all_to_all(
        sent.reshape(seq_count, capacity, 2, BLK, HD), "seq", split_axis=0, concat_axis=0, tiled=True
    ).reshape(slot_total, 2, BLK, HD)

    steps = [(d, e) for d in range(chips) for e in range(CORES)]
    step_chip = jnp.array([d for d, _ in steps], jnp.int32)
    step_core = jnp.array([e for _, e in steps], jnp.int32)
    ahead = (chip + step_chip) % chips * CORES + (core + step_core) % CORES
    pieces = split_queries(queries, ahead)
    rows_of = {}
    for piece, (d, e) in zip(pieces, steps):
        rows_of[d, e] = piece if d == e == 0 else lax.ppermute(piece, "head", offset_pairs(chips, d, e))

    order = (chip - jnp.arange(chips, dtype=jnp.int32)) % chips
    near_ids = jnp.take((block_ids[:, :NEAR] - seq_place * k_count).reshape(chips, per_chip, NEAR), order, axis=0)
    slots = jnp.take(far_slot.reshape(chips, per_chip, far_count), order, axis=0)
    core_operand = core.astype(jnp.int32).reshape(1)

    near = [
        near_attention(near_ids[d], core_operand, rows_of[d, 0], rows_of[d, 1], cache_keys, cache_values)
        for d in range(chips)
    ]
    got, near = lax.optimization_barrier((got, near))
    results = {}
    for d in sorted(range(chips), key=lambda d: -min(d, chips - d)):
        made = far_attention(slots[d], core_operand, got, *near[d])
        for e in range(CORES):
            results[d, e] = made[e] if d == e == 0 else lax.ppermute(made[e], "head", offset_pairs(chips, -d, e))
    return join_outputs([results[step] for step in steps], ahead)


def solution(mesh):
    return jax.shard_map(
        shards,
        mesh=mesh,
        in_specs=(P(("seq", "head"), None), P("seq", "head"), P("seq", "head"), P("seq", None)),
        out_specs=P(("seq", "head"), None),
        check_vma=False,
    )
```

```python
import functools

import jax
import jax.numpy as jnp
from jax import lax
from jax.experimental import pallas as pl
from jax.experimental.pallas import tpu as pltpu
from jax.sharding import PartitionSpec as P

HD = 128
BLK = 128
NEAR = 5
CORES = 2
HBM = pl.BlockSpec(memory_space=pltpu.HBM)
SMEM = pl.BlockSpec(memory_space=pltpu.SMEM)
VMEM = pl.BlockSpec(memory_space=pltpu.VMEM)
LOG2E = 1.4426950408889634


def wait_for(ref, sem):
    pltpu.make_async_copy(ref, ref, sem).wait()


def room(mebibytes):
    return pltpu.CompilerParams(vmem_limit_bytes=mebibytes * 1024 * 1024)


def cost(flops, bytes_accessed, transcendentals=0):
    return pl.CostEstimate(flops=flops, bytes_accessed=bytes_accessed, transcendentals=transcendentals)


def split_queries_kernel(places_ref, q_ref, *refs):
    count = len(refs) - 3
    outs, buf, in_sem, out_sem = refs[:count], *refs[count:]
    width = buf.shape[2]
    into, out_of = [], []
    for i in range(count):
        start = pl.multiple_of(places_ref[i] * width, width)
        into.append(pltpu.make_async_copy(q_ref.at[:, pl.ds(start, width)], buf.at[i], in_sem.at[i]))
        out_of.append(pltpu.make_async_copy(buf.at[i], outs[i], out_sem.at[i]))
    for copy in into:
        copy.start()
    for i in range(count):
        into[i].wait()
        out_of[i].start()
    for copy in out_of:
        copy.wait()


def split_queries(queries, places):
    count = places.shape[0]
    rows, width = queries.shape[0], queries.shape[1] // count
    return pl.pallas_call(
        split_queries_kernel,
        out_shape=[jax.ShapeDtypeStruct((rows, width), queries.dtype)] * count,
        in_specs=[SMEM, HBM],
        out_specs=[HBM] * count,
        scratch_shapes=[
            pltpu.VMEM((count, rows, width), queries.dtype),
            pltpu.SemaphoreType.DMA((count,)),
            pltpu.SemaphoreType.DMA((count,)),
        ],
        cost_estimate=cost(0, 4 * queries.size),
    )(places, queries)


def join_outputs_kernel(places_ref, *refs):
    count = len(refs) - 2
    pieces, out_ref, sem = refs[:count], refs[count], refs[count + 1]
    width = pieces[0].shape[2]
    copies = []
    for i in range(count):
        start = pl.multiple_of(places_ref[i] * width, width)
        copies.append(pltpu.make_async_copy(pieces[i].at[i % CORES], out_ref.at[:, pl.ds(start, width)], sem.at[i]))
    for copy in copies:
        copy.start()
    for copy in copies:
        copy.wait()


def join_outputs(pieces, places):
    count = len(pieces)
    _, rows, width = pieces[0].shape
    return pl.pallas_call(
        join_outputs_kernel,
        out_shape=jax.ShapeDtypeStruct((rows, width * count), pieces[0].dtype),
        in_specs=[SMEM] + [VMEM] * count,
        out_specs=HBM,
        scratch_shapes=[pltpu.SemaphoreType.DMA((count,))],
        compiler_params=room(6),
        cost_estimate=cost(0, 4 * rows * width * count),
    )(places, *pieces)


def pack_kernel(chunks, ahead, wanted_ref, k_ref, v_ref, out_ref, buf, in_sem, out_sem):
    span, capacity = out_ref.shape[0] // chunks, wanted_ref.shape[2]

    def fetch(chunk):
        for i in range(chunk * span, (chunk + 1) * span):
            rows = pl.ds(pl.multiple_of(wanted_ref[i // capacity, 0, i % capacity] * BLK, BLK), BLK)
            pltpu.make_async_copy(k_ref.at[rows], buf.at[i, 0], in_sem.at[chunk]).start()
            pltpu.make_async_copy(v_ref.at[rows], buf.at[i, 1], in_sem.at[chunk]).start()

    copies = []
    for chunk in range(min(ahead, chunks)):
        fetch(chunk)
    for chunk in range(chunks):
        part = pl.ds(chunk * span, span)
        wait_for(buf.at[part], in_sem.at[chunk])
        copies.append(pltpu.make_async_copy(buf.at[part], out_ref.at[part], out_sem.at[chunk]))
        copies[-1].start()
        if chunk + ahead < chunks:
            fetch(chunk + ahead)
    for copy in copies:
        copy.wait()


def pack(wanted, keys, values, chunks=8, ahead=2):
    count = wanted.shape[0] * wanted.shape[2]
    return pl.pallas_call(
        functools.partial(pack_kernel, chunks, ahead),
        out_shape=jax.ShapeDtypeStruct((count, 2, BLK, HD), keys.dtype),
        in_specs=[SMEM, HBM, HBM],
        out_specs=HBM,
        scratch_shapes=[
            pltpu.VMEM((count, 2, BLK, HD), keys.dtype),
            pltpu.SemaphoreType.DMA((chunks,)),
            pltpu.SemaphoreType.DMA((chunks,)),
        ],
        cost_estimate=cost(0, 8 * count * BLK * HD),
    )(wanted, keys, values)


def scores_of(keys, queries):
    return lax.dot_general(keys, queries, (((1,), (1,)), ((), ())), preferred_element_type=jnp.float32)


def weighted(values, weights):
    return lax.dot_general(values, weights, (((0,), (0,)), ((), ())), preferred_element_type=jnp.float32)


def near_kernel(first, ids_ref, core_ref, qa_ref, qb_ref, k_ref, v_ref, acc_out, stat_out, q_out, q_buf, k_buf, v_buf, acc_ref, stat_ref, q_ref, k_sem, v_sem, out_sem):
    blocks, picks, half = acc_ref.shape[0], k_buf.shape[1] // BLK, qa_ref.shape[0]
    ratio = q_buf.shape[1] // HD
    factor = HD ** (-0.5) * LOG2E
    core = core_ref[0]
    for i in range(blocks):
        for j in range(picks):
            held = pl.ds(pl.multiple_of(ids_ref[first + i, j] * BLK, BLK), BLK)
            pltpu.make_async_copy(k_ref.at[held], k_buf.at[i, pl.ds(j * BLK, BLK)], k_sem.at[i]).start()
            pltpu.make_async_copy(v_ref.at[held], v_buf.at[i, pl.ds(j * BLK, BLK)], v_sem.at[i]).start()
    q_buf[pl.ds(pl.multiple_of(core * half, half), half), :] = qa_ref[...]
    q_buf[pl.ds(pl.multiple_of((1 - core) * half, half), half), :] = qb_ref[...]
    for i in range(blocks):
        for r in range(ratio):
            q_ref[i, r * BLK : (r + 1) * BLK, :] = q_buf[i * BLK : (i + 1) * BLK, r * HD : (r + 1) * HD]
    copies = [pltpu.make_async_copy(q_ref, q_out, out_sem.at[0])]
    copies[0].start()

    def block(i, carry):
        wait_for(k_buf.at[i], k_sem.at[i])
        wait_for(v_buf.at[i], v_sem.at[i])
        score = scores_of(k_buf[i], q_ref[i])
        highest = jnp.max(score, axis=0, keepdims=True) * factor
        exponent = jnp.exp2(score * factor - highest)
        stat_ref[i, 0:1, :] = highest
        stat_ref[i, 1:2, :] = jnp.sum(exponent, axis=0, keepdims=True)
        acc_ref[i] = weighted(v_buf[i], exponent.astype(jnp.bfloat16))
        return carry

    lax.fori_loop(0, blocks, block, 0)
    copies.append(pltpu.make_async_copy(acc_ref, acc_out, out_sem.at[1]))
    copies.append(pltpu.make_async_copy(stat_ref, stat_out, out_sem.at[2]))
    copies[1].start()
    copies[2].start()
    for copy in copies:
        copy.wait()


def near_attention(ids, first, core, qa, qb, keys, values):
    picks = ids.shape[1]
    rows, width = 2 * qa.shape[0], qa.shape[1]
    blocks = rows // BLK
    span, wide = picks * BLK, BLK * (width // HD)
    work = rows * width * span
    kept = [((blocks, HD, wide), jnp.float32), ((blocks, 8, wide), jnp.float32), ((blocks, wide, HD), qa.dtype)]
    return pl.pallas_call(
        functools.partial(near_kernel, first),
        out_shape=[jax.ShapeDtypeStruct(*what) for what in kept],
        in_specs=[SMEM, SMEM, VMEM, VMEM, HBM, HBM],
        out_specs=[HBM] * 3,
        scratch_shapes=[
            pltpu.VMEM((rows, width), qa.dtype),
            pltpu.VMEM((blocks, span, HD), keys.dtype),
            pltpu.VMEM((blocks, span, HD), keys.dtype),
            *[pltpu.VMEM(*what) for what in kept],
            pltpu.SemaphoreType.DMA((blocks,)),
            pltpu.SemaphoreType.DMA((blocks,)),
            pltpu.SemaphoreType.DMA((3,)),
        ],
        cost_estimate=cost(4 * work, 8 * rows * width + 4 * blocks * span * HD, work // HD),
    )(ids, core, qa, qb, keys, values)


def far_kernel(firsts, slots_ref, core_ref, got_ref, *refs):
    groups = len(firsts)
    kept_in, o_refs = refs[: 3 * groups], refs[3 * groups : 4 * groups]
    k_buf, v_buf, acc_ref, stat_ref, q_ref, o_buf, k_sem, v_sem, in_sem, out_sem = refs[4 * groups :]
    picks, half = k_buf.shape[1] // BLK, o_buf.shape[2]
    ratio, blocks = o_buf.shape[3] // HD, k_buf.shape[0] // groups
    factor = HD ** (-0.5) * LOG2E
    core = core_ref[0]
    eye = lax.broadcasted_iota(jnp.int32, (HD, HD), 0) == lax.broadcasted_iota(jnp.int32, (HD, HD), 1)
    eye = eye.astype(jnp.float32).astype(jnp.bfloat16)

    def kept_copies(n):
        g, i = divmod(n, blocks)
        acc_in, stat_in, q_in = kept_in[3 * g : 3 * g + 3]
        return (
            pltpu.make_async_copy(q_in.at[i], q_ref.at[n], in_sem.at[n, 0]),
            pltpu.make_async_copy(stat_in.at[i], stat_ref.at[n], in_sem.at[n, 1]),
            pltpu.make_async_copy(acc_in.at[i], acc_ref.at[n], in_sem.at[n, 2]),
        )

    def fetch(n):
        g, i = divmod(n, blocks)
        copies = kept_copies(n)
        copies[0].start()
        for side, (buf, sem) in enumerate(((k_buf, k_sem), (v_buf, v_sem))):
            for j in range(picks):
                source = got_ref.at[slots_ref[firsts[g] + i, j], side]
                pltpu.make_async_copy(source, buf.at[n, pl.ds(j * BLK, BLK)], sem.at[n]).start()
        copies[1].start()
        copies[2].start()

    sent = []
    for n in range(2):
        fetch(n)
    for n in range(groups * blocks):
        g, i = divmod(n, blocks)
        if n + 2 < groups * blocks:
            fetch(n + 2)
        copies = kept_copies(n)
        copies[0].wait()
        wait_for(k_buf.at[n], k_sem.at[n])
        score = scores_of(k_buf[n], q_ref[n])
        copies[1].wait()
        before = stat_ref[n, 0:1, :]
        highest = jnp.maximum(jnp.max(score, axis=0, keepdims=True) * factor, before)
        exponent = jnp.exp2(score * factor - highest)
        kept = jnp.exp2(before - highest)
        total = jnp.sum(exponent, axis=0, keepdims=True) + kept * stat_ref[n, 1:2, :]
        wait_for(v_buf.at[n], v_sem.at[n])
        partial = weighted(v_buf[n], exponent.astype(jnp.bfloat16))
        copies[2].wait()
        merged = ((partial + kept * acc_ref[n]) * (1.0 / total)).astype(o_buf.dtype)
        for r in range(ratio):
            turned = scores_of(eye, merged[:, r * BLK : (r + 1) * BLK]).astype(o_buf.dtype)
            for part in range(CORES):
                low, high = max(i * BLK, part * half), min((i + 1) * BLK, (part + 1) * half)
                if low < high:
                    o_buf[g, part, low - part * half : high - part * half, r * HD : (r + 1) * HD] = turned[
                        low - i * BLK : high - i * BLK
                    ]
        for part in range(CORES):
            if -(-(part + 1) * half // BLK) == i + 1:
                place = core if part == 0 else 1 - core
                sent.append(pltpu.make_async_copy(o_buf.at[g, part], o_refs[g].at[place], out_sem.at[g, part]))
                sent[-1].start()
    for copy in sent:
        copy.wait()


def far_attention(slots, firsts, core, got, kept):
    groups, picks = len(firsts), slots.shape[1]
    acc, stats, q = kept[0]
    blocks, wide = q.shape[0], q.shape[1]
    count = groups * blocks
    half, width = blocks * BLK // CORES, wide // BLK * HD
    span = picks * BLK
    work = count * BLK * width * span
    return pl.pallas_call(
        functools.partial(far_kernel, firsts),
        out_shape=[jax.ShapeDtypeStruct((CORES, half, width), q.dtype)] * groups,
        in_specs=[SMEM, SMEM] + [HBM] * (1 + 3 * groups),
        out_specs=[HBM] * groups,
        scratch_shapes=[
            pltpu.VMEM((count, span, HD), got.dtype),
            pltpu.VMEM((count, span, HD), got.dtype),
            pltpu.VMEM((count,) + acc.shape[1:], acc.dtype),
            pltpu.VMEM((count,) + stats.shape[1:], stats.dtype),
            pltpu.VMEM((count,) + q.shape[1:], q.dtype),
            pltpu.VMEM((groups, CORES, half, width), q.dtype),
            pltpu.SemaphoreType.DMA((count,)),
            pltpu.SemaphoreType.DMA((count,)),
            pltpu.SemaphoreType.DMA((count, 3)),
            pltpu.SemaphoreType.DMA((groups, CORES)),
        ],
        cost_estimate=cost(4 * work, 4 * count * (2 * BLK * width + span * HD), work // HD),
    )(slots, core, got, *[array for group in kept for array in group])


def offset_pairs(chips, chip_step, core_step):
    return [
        (chip * CORES + core, (chip + chip_step) % chips * CORES + (core ^ core_step))
        for chip in range(chips)
        for core in range(CORES)
    ]


def shards(queries, cache_keys, cache_values, block_ids):
    seq_count = lax.axis_size("seq")
    heads = lax.axis_size("head")
    seq_place = lax.axis_index("seq")
    head_place = lax.axis_index("head")
    chips = heads // CORES
    chip, core = head_place // CORES, head_place % CORES
    q_count, k_count = block_ids.shape[0], cache_keys.shape[0] // BLK
    per_chip = q_count // chips
    far_count = block_ids.shape[1] - NEAR
    capacity = max(2, (far_count * q_count + seq_count - 2) // (seq_count - 1))
    slot_total = seq_count * capacity

    far_ids = block_ids[:, NEAR:].reshape(-1)
    far_owner = far_ids // k_count
    far_within = far_ids - far_owner * k_count
    entry = jnp.arange(far_ids.shape[0], dtype=jnp.int32)
    earlier = (far_owner[:, None] == far_owner[None, :]) & (entry[None, :] < entry[:, None])
    far_slot = far_owner * capacity + jnp.sum(earlier.astype(jnp.int32), axis=1)
    slot_range = jnp.arange(slot_total, dtype=jnp.int32)
    unasked = slot_range % k_count
    placed = far_slot[:, None] == slot_range[None, :]
    asked = unasked + jnp.sum(jnp.where(placed, far_within[:, None] - unasked[None, :], 0), axis=0)
    wanted = lax.all_to_all(asked.reshape(seq_count, 1, capacity), "seq", split_axis=0, concat_axis=0, tiled=True)

    sent = pack(wanted, cache_keys, cache_values)
    got = lax.all_to_all(
        sent.reshape(seq_count, capacity, 2, BLK, HD), "seq", split_axis=0, concat_axis=0, tiled=True
    ).reshape(slot_total, 2, BLK, HD)

    steps = [(d, e) for d in range(chips) for e in range(CORES)]
    step_chip = jnp.array([d for d, _ in steps], jnp.int32)
    step_core = jnp.array([e for _, e in steps], jnp.int32)
    ahead = (chip + step_chip) % chips * CORES + (core + step_core) % CORES
    pieces = split_queries(queries, ahead)
    rows_of = {}
    for piece, (d, e) in zip(pieces, steps):
        rows_of[d, e] = piece if d == e == 0 else lax.ppermute(piece, "head", offset_pairs(chips, d, e))

    order = (chip - jnp.arange(chips, dtype=jnp.int32)) % chips
    own_ids = jnp.concatenate([block_ids[:, :NEAR] - seq_place * k_count, far_slot.reshape(q_count, far_count)], axis=1)
    own_ids = jnp.take(own_ids.reshape(chips, per_chip, -1), order, axis=0).reshape(q_count, -1)
    near_ids, slots = own_ids[:, :NEAR], own_ids[:, NEAR:]
    core_operand = core.astype(jnp.int32).reshape(1)
    near = [
        near_attention(near_ids, d * per_chip, core_operand, rows_of[d, 0], rows_of[d, 1], cache_keys, cache_values)
        for d in range(chips)
    ]
    got, near, slots = lax.optimization_barrier((got, near, slots))

    results = [None] * chips
    distance = lambda d: min(d, chips - d)
    for hops in range(chips // 2, -1, -1):
        group = [d for d in range(chips) if distance(d) == hops]
        made = far_attention(slots, tuple(d * per_chip for d in group), core_operand, got, [near[d] for d in group])
        if hops:
            made, got = lax.optimization_barrier((made, got))
        for d, rows in zip(group, made):
            results[d] = lax.ppermute(rows, "head", offset_pairs(chips, -d, 0)) if d else rows
    joined = []
    for d in range(chips):
        joined += [results[d], lax.ppermute(results[d], "head", offset_pairs(chips, 0, 1))]
    return join_outputs(joined, ahead)


def solution(mesh):
    return jax.shard_map(
        shards,
        mesh=mesh,
        in_specs=(P(("seq", "head"), None), P("seq", "head"), P("seq", "head"), P("seq", None)),
        out_specs=P(("seq", "head"), None),
        check_vma=False,
    )
```

```python
import functools

import jax
import jax.numpy as jnp
from jax import lax
from jax.experimental import pallas as pl
from jax.experimental.pallas import tpu as pltpu
from jax.sharding import PartitionSpec as P

HD = 128
BLK = 128
NEAR = 5
CORES = 2
HBM = pl.BlockSpec(memory_space=pltpu.HBM)
SMEM = pl.BlockSpec(memory_space=pltpu.SMEM)
VMEM = pl.BlockSpec(memory_space=pltpu.VMEM)
LOG2E = 1.4426950408889634
HIGHEST, TOTAL, KEPT_ROWS = HD, HD + 1, HD + 8


def wait_for(ref, sem):
    pltpu.make_async_copy(ref, ref, sem).wait()


def room(mebibytes):
    return pltpu.CompilerParams(vmem_limit_bytes=mebibytes * 1024 * 1024)


def cost(flops, bytes_accessed, transcendentals=0):
    return pl.CostEstimate(flops=flops, bytes_accessed=bytes_accessed, transcendentals=transcendentals)


def split_queries_kernel(places_ref, q_ref, *refs):
    count = len(refs) - 3
    outs, buf, in_sem, out_sem = refs[:count], *refs[count:]
    width = buf.shape[2]
    into, out_of = [], []
    for i in range(count):
        start = pl.multiple_of(places_ref[i] * width, width)
        into.append(pltpu.make_async_copy(q_ref.at[:, pl.ds(start, width)], buf.at[i], in_sem.at[i]))
        out_of.append(pltpu.make_async_copy(buf.at[i], outs[i], out_sem.at[i]))
    for copy in into:
        copy.start()
    for i in range(count):
        into[i].wait()
        out_of[i].start()
    for copy in out_of:
        copy.wait()


def split_queries(queries, places):
    count = places.shape[0]
    rows, width = queries.shape[0], queries.shape[1] // count
    return pl.pallas_call(
        split_queries_kernel,
        out_shape=[jax.ShapeDtypeStruct((rows, width), queries.dtype)] * count,
        in_specs=[SMEM, HBM],
        out_specs=[HBM] * count,
        scratch_shapes=[
            pltpu.VMEM((count, rows, width), queries.dtype),
            pltpu.SemaphoreType.DMA((count,)),
            pltpu.SemaphoreType.DMA((count,)),
        ],
        cost_estimate=cost(0, 4 * queries.size),
    )(places, queries)


def join_outputs_kernel(places_ref, *refs):
    count = len(refs) - 2
    pieces, out_ref, sem = refs[:count], refs[count], refs[count + 1]
    width = pieces[0].shape[2]
    copies = []
    for i in range(count):
        start = pl.multiple_of(places_ref[i] * width, width)
        copies.append(pltpu.make_async_copy(pieces[i].at[i % CORES], out_ref.at[:, pl.ds(start, width)], sem.at[i]))
    for copy in copies:
        copy.start()
    for copy in copies:
        copy.wait()


def join_outputs(pieces, places):
    count = len(pieces)
    _, rows, width = pieces[0].shape
    return pl.pallas_call(
        join_outputs_kernel,
        out_shape=jax.ShapeDtypeStruct((rows, width * count), pieces[0].dtype),
        in_specs=[SMEM] + [VMEM] * count,
        out_specs=HBM,
        scratch_shapes=[pltpu.SemaphoreType.DMA((count,))],
        compiler_params=room(6),
        cost_estimate=cost(0, 4 * rows * width * count),
    )(places, *pieces)


def pack_kernel(chunks, ahead, wanted_ref, k_ref, v_ref, out_ref, buf, in_sem, out_sem):
    span, capacity = out_ref.shape[0] // chunks, wanted_ref.shape[2]

    def fetch(chunk):
        for i in range(chunk * span, (chunk + 1) * span):
            rows = pl.ds(pl.multiple_of(wanted_ref[i // capacity, 0, i % capacity] * BLK, BLK), BLK)
            pltpu.make_async_copy(k_ref.at[rows], buf.at[i, 0], in_sem.at[chunk]).start()
            pltpu.make_async_copy(v_ref.at[rows], buf.at[i, 1], in_sem.at[chunk]).start()

    copies = []
    for chunk in range(min(ahead, chunks)):
        fetch(chunk)
    for chunk in range(chunks):
        part = pl.ds(chunk * span, span)
        wait_for(buf.at[part], in_sem.at[chunk])
        copies.append(pltpu.make_async_copy(buf.at[part], out_ref.at[part], out_sem.at[chunk]))
        copies[-1].start()
        if chunk + ahead < chunks:
            fetch(chunk + ahead)
    for copy in copies:
        copy.wait()


def pack(wanted, keys, values, chunks=4, ahead=4):
    count = wanted.shape[0] * wanted.shape[2]
    return pl.pallas_call(
        functools.partial(pack_kernel, chunks, ahead),
        out_shape=jax.ShapeDtypeStruct((count, 2, BLK, HD), keys.dtype),
        in_specs=[SMEM, HBM, HBM],
        out_specs=HBM,
        scratch_shapes=[
            pltpu.VMEM((count, 2, BLK, HD), keys.dtype),
            pltpu.SemaphoreType.DMA((chunks,)),
            pltpu.SemaphoreType.DMA((chunks,)),
        ],
        cost_estimate=cost(0, 8 * count * BLK * HD),
    )(wanted, keys, values)


def scores_of(keys, queries):
    return lax.dot_general(keys, queries, (((1,), (1,)), ((), ())), preferred_element_type=jnp.float32)


def weighted(values, weights):
    return lax.dot_general(values, weights, (((0,), (0,)), ((), ())), preferred_element_type=jnp.float32)


def near_kernel(first, ids_ref, core_ref, qa_ref, qb_ref, k_ref, v_ref, kept_out, q_out, q_buf, k_buf, v_buf, kept_ref, q_ref, k_sem, v_sem, out_sem):
    blocks, picks, half = q_ref.shape[0], k_buf.shape[1] // BLK, qa_ref.shape[0]
    ratio = q_buf.shape[1] // HD
    factor = HD ** (-0.5) * LOG2E
    core = core_ref[0]
    for i in range(blocks):
        for j in range(picks):
            held = pl.ds(pl.multiple_of(ids_ref[first + i, j] * BLK, BLK), BLK)
            pltpu.make_async_copy(k_ref.at[held], k_buf.at[i, pl.ds(j * BLK, BLK)], k_sem.at[i]).start()
            pltpu.make_async_copy(v_ref.at[held], v_buf.at[i, pl.ds(j * BLK, BLK)], v_sem.at[i]).start()
    q_buf[pl.ds(pl.multiple_of(core * half, half), half), :] = qa_ref[...]
    q_buf[pl.ds(pl.multiple_of((1 - core) * half, half), half), :] = qb_ref[...]
    for i in range(blocks):
        for r in range(ratio):
            q_ref[i, r * BLK : (r + 1) * BLK, :] = q_buf[i * BLK : (i + 1) * BLK, r * HD : (r + 1) * HD]
    q_copy = pltpu.make_async_copy(q_ref, q_out, out_sem.at[0])
    q_copy.start()

    def block(i, carry):
        wait_for(k_buf.at[i], k_sem.at[i])
        wait_for(v_buf.at[i], v_sem.at[i])
        score = scores_of(k_buf[i], q_ref[i])
        highest = jnp.max(score, axis=0, keepdims=True) * factor
        exponent = jnp.exp2(score * factor - highest)
        kept_ref[i, HIGHEST : HIGHEST + 1, :] = highest
        kept_ref[i, TOTAL : TOTAL + 1, :] = jnp.sum(exponent, axis=0, keepdims=True)
        kept_ref[i, 0:HD, :] = weighted(v_buf[i], exponent.astype(jnp.bfloat16))
        return carry

    lax.fori_loop(0, blocks, block, 0)
    kept_copy = pltpu.make_async_copy(kept_ref, kept_out, out_sem.at[1])
    kept_copy.start()
    q_copy.wait()
    kept_copy.wait()


def near_attention(ids, first, core, qa, qb, keys, values):
    picks = ids.shape[1]
    rows, width = 2 * qa.shape[0], qa.shape[1]
    blocks = rows // BLK
    span, wide = picks * BLK, BLK * (width // HD)
    work = rows * width * span
    kept = [((blocks, KEPT_ROWS, wide), jnp.float32), ((blocks, wide, HD), qa.dtype)]
    return pl.pallas_call(
        functools.partial(near_kernel, first),
        out_shape=[jax.ShapeDtypeStruct(*what) for what in kept],
        in_specs=[SMEM, SMEM, VMEM, VMEM, HBM, HBM],
        out_specs=[HBM] * 2,
        scratch_shapes=[
            pltpu.VMEM((rows, width), qa.dtype),
            pltpu.VMEM((blocks, span, HD), keys.dtype),
            pltpu.VMEM((blocks, span, HD), keys.dtype),
            *[pltpu.VMEM(*what) for what in kept],
            pltpu.SemaphoreType.DMA((blocks,)),
            pltpu.SemaphoreType.DMA((blocks,)),
            pltpu.SemaphoreType.DMA((2,)),
        ],
        cost_estimate=cost(4 * work, 8 * rows * width + 4 * blocks * span * HD, work // HD),
    )(ids, core, qa, qb, keys, values)


def far_kernel(firsts, slots_ref, core_ref, got_ref, *refs):
    groups = len(firsts)
    near_refs, o_refs = refs[: 2 * groups], refs[2 * groups : 3 * groups]
    far_buf, far_sem = refs[3 * groups :]
    picks, half = far_buf.shape[1], o_refs[0].shape[1]
    ratio, blocks = o_refs[0].shape[2] // HD, far_buf.shape[0] // groups
    factor = HD ** (-0.5) * LOG2E
    core = core_ref[0]
    for n in range(groups * blocks):
        g, i = divmod(n, blocks)
        for j in range(picks):
            pltpu.make_async_copy(got_ref.at[slots_ref[firsts[g] + i, j]], far_buf.at[n, j], far_sem.at[n]).start()
    for n in range(groups * blocks):
        g, i = divmod(n, blocks)
        kept_ref, q_ref = near_refs[2 * g : 2 * g + 2]
        wait_for(far_buf.at[n], far_sem.at[n])
        score = scores_of(jnp.concatenate([far_buf[n, j, 0] for j in range(picks)], axis=0), q_ref[i])
        before = kept_ref[i, HIGHEST : HIGHEST + 1, :]
        highest = jnp.maximum(jnp.max(score, axis=0, keepdims=True) * factor, before)
        exponent = jnp.exp2(score * factor - highest)
        kept = jnp.exp2(before - highest)
        total = jnp.sum(exponent, axis=0, keepdims=True) + kept * kept_ref[i, TOTAL : TOTAL + 1, :]
        partial = weighted(
            jnp.concatenate([far_buf[n, j, 1] for j in range(picks)], axis=0), exponent.astype(jnp.bfloat16)
        )
        merged = (partial + kept * kept_ref[i, 0:HD, :]) * (1.0 / total)
        for r in range(ratio):
            turned = merged[:, r * BLK : (r + 1) * BLK].T.astype(o_refs[g].dtype)
            for part in range(CORES):
                low, high = max(i * BLK, part * half), min((i + 1) * BLK, (part + 1) * half)
                if low < high:
                    place = core if part == 0 else 1 - core
                    rows = slice(low - part * half, high - part * half)
                    o_refs[g][place, rows, r * HD : (r + 1) * HD] = turned[low - i * BLK : high - i * BLK]


def far_attention(slots, firsts, core, got, near):
    groups, picks = len(firsts), slots.shape[1]
    _, q = near[0]
    blocks, wide = q.shape[0], q.shape[1]
    count = groups * blocks
    half, width = blocks * BLK // CORES, wide // BLK * HD
    return pl.pallas_call(
        functools.partial(far_kernel, firsts),
        out_shape=[jax.ShapeDtypeStruct((CORES, half, width), q.dtype)] * groups,
        in_specs=[SMEM, SMEM, HBM] + [VMEM] * (2 * groups),
        out_specs=[VMEM] * groups,
        scratch_shapes=[pltpu.VMEM((count, picks) + got.shape[1:], got.dtype), pltpu.SemaphoreType.DMA((count,))],
        compiler_params=room(16),
        cost_estimate=cost(1, 1),
    )(slots, core, got, *[array for group in near for array in group])


def offset_pairs(chips, chip_step, core_step):
    return [
        (chip * CORES + core, (chip + chip_step) % chips * CORES + (core ^ core_step))
        for chip in range(chips)
        for core in range(CORES)
    ]


def shards(queries, cache_keys, cache_values, block_ids):
    seq_count = lax.axis_size("seq")
    heads = lax.axis_size("head")
    seq_place = lax.axis_index("seq")
    head_place = lax.axis_index("head")
    chips = heads // CORES
    chip, core = head_place // CORES, head_place % CORES
    q_count, k_count = block_ids.shape[0], cache_keys.shape[0] // BLK
    per_chip = q_count // chips
    far_count = block_ids.shape[1] - NEAR
    capacity = max(2, (far_count * q_count + seq_count - 2) // (seq_count - 1))
    slot_total = seq_count * capacity

    far_ids = block_ids[:, NEAR:].reshape(-1)
    far_owner = far_ids // k_count
    far_within = far_ids - far_owner * k_count
    entry = jnp.arange(far_ids.shape[0], dtype=jnp.int32)
    earlier = (far_owner[:, None] == far_owner[None, :]) & (entry[None, :] < entry[:, None])
    far_slot = far_owner * capacity + jnp.sum(earlier.astype(jnp.int32), axis=1)
    slot_range = jnp.arange(slot_total, dtype=jnp.int32)
    unasked = slot_range % k_count
    placed = far_slot[:, None] == slot_range[None, :]
    asked = unasked + jnp.sum(jnp.where(placed, far_within[:, None] - unasked[None, :], 0), axis=0)
    wanted = lax.all_to_all(asked.reshape(seq_count, 1, capacity), "seq", split_axis=0, concat_axis=0, tiled=True)

    sent = pack(wanted, cache_keys, cache_values)
    got = lax.all_to_all(
        sent.reshape(seq_count, capacity, 2, BLK, HD), "seq", split_axis=0, concat_axis=0, tiled=True
    ).reshape(slot_total, 2, BLK, HD)

    steps = [(d, e) for d in range(chips) for e in range(CORES)]
    step_chip = jnp.array([d for d, _ in steps], jnp.int32)
    step_core = jnp.array([e for _, e in steps], jnp.int32)
    ahead = (chip + step_chip) % chips * CORES + (core + step_core) % CORES
    pieces = split_queries(queries, ahead)
    rows_of = {}
    for piece, (d, e) in zip(pieces, steps):
        rows_of[d, e] = piece if d == e == 0 else lax.ppermute(piece, "head", offset_pairs(chips, d, e))

    order = (chip - jnp.arange(chips, dtype=jnp.int32)) % chips
    own_ids = jnp.concatenate([block_ids[:, :NEAR] - seq_place * k_count, far_slot.reshape(q_count, far_count)], axis=1)
    own_ids = jnp.take(own_ids.reshape(chips, per_chip, -1), order, axis=0).reshape(q_count, -1)
    near_ids, slots = own_ids[:, :NEAR], own_ids[:, NEAR:]
    core_operand = core.astype(jnp.int32).reshape(1)
    near = [
        near_attention(near_ids, d * per_chip, core_operand, rows_of[d, 0], rows_of[d, 1], cache_keys, cache_values)
        for d in range(chips)
    ]
    got, near, slots = lax.optimization_barrier((got, near, slots))

    results = [None] * chips
    distance = lambda d: min(d, chips - d)
    for hops in range(chips // 2, -1, -1):
        group = [d for d in range(chips) if distance(d) == hops]
        if not hops:
            got, results[chips // 2] = lax.optimization_barrier((got, results[chips // 2]))
        made = far_attention(slots, tuple(d * per_chip for d in group), core_operand, got, [near[d] for d in group])
        if hops:
            made, got = lax.optimization_barrier((made, got))
        for d, rows in zip(group, made):
            results[d] = lax.ppermute(rows, "head", offset_pairs(chips, -d, 0)) if d else rows
    joined = []
    for d in range(chips):
        joined += [results[d], lax.ppermute(results[d], "head", offset_pairs(chips, 0, 1))]
    return join_outputs(joined, ahead)


def solution(mesh):
    return jax.shard_map(
        shards,
        mesh=mesh,
        in_specs=(P(("seq", "head"), None), P("seq", "head"), P("seq", "head"), P("seq", None)),
        out_specs=P(("seq", "head"), None),
        check_vma=False,
    )
```

```python
import functools

import jax
import jax.numpy as jnp
from jax import lax
from jax.experimental import pallas as pl
from jax.experimental.pallas import tpu as pltpu
from jax.sharding import PartitionSpec as P

HD = 128
BLK = 128
NEAR = 5
CORES = 2
HBM = pl.BlockSpec(memory_space=pltpu.HBM)
SMEM = pl.BlockSpec(memory_space=pltpu.SMEM)
VMEM = pl.BlockSpec(memory_space=pltpu.VMEM)
LOG2E = 1.4426950408889634
HIGHEST, TOTAL, KEPT_ROWS = HD, HD + 1, HD + 8


def wait_for(ref, sem):
    pltpu.make_async_copy(ref, ref, sem).wait()


def room(mebibytes):
    return pltpu.CompilerParams(vmem_limit_bytes=mebibytes * 1024 * 1024)


def cost(flops, bytes_accessed, transcendentals=0):
    return pl.CostEstimate(flops=flops, bytes_accessed=bytes_accessed, transcendentals=transcendentals)


def split_queries_kernel(places_ref, q_ref, *refs):
    count = len(refs) - 3
    outs, buf, in_sem, out_sem = refs[:count], *refs[count:]
    width = buf.shape[2]
    into, out_of = [], []
    for i in range(count):
        start = pl.multiple_of(places_ref[i] * width, width)
        into.append(pltpu.make_async_copy(q_ref.at[:, pl.ds(start, width)], buf.at[i], in_sem.at[i]))
        out_of.append(pltpu.make_async_copy(buf.at[i], outs[i], out_sem.at[i]))
    for copy in into:
        copy.start()
    for i in range(count):
        into[i].wait()
        out_of[i].start()
    for copy in out_of:
        copy.wait()


def split_queries(queries, places):
    count = places.shape[0]
    rows, width = queries.shape[0], queries.shape[1] // count
    return pl.pallas_call(
        split_queries_kernel,
        out_shape=[jax.ShapeDtypeStruct((rows, width), queries.dtype)] * count,
        in_specs=[SMEM, HBM],
        out_specs=[HBM] * count,
        scratch_shapes=[
            pltpu.VMEM((count, rows, width), queries.dtype),
            pltpu.SemaphoreType.DMA((count,)),
            pltpu.SemaphoreType.DMA((count,)),
        ],
        cost_estimate=cost(0, 4 * queries.size),
    )(places, queries)


def join_outputs_kernel(count, chosen, places_ref, *refs):
    pieces, out_ref, sem = refs[: len(chosen)], refs[-2], refs[-1]
    width = out_ref.shape[1] // count
    copies = []
    for piece, i in zip(pieces, chosen):
        start = pl.multiple_of(places_ref[i] * width, width)
        copies.append(pltpu.make_async_copy(piece.at[i % CORES], out_ref.at[:, pl.ds(start, width)], sem.at[i]))
    for copy in copies:
        copy.start()
    for copy in copies:
        copy.wait()


def join_outputs(pieces, chosen, places, out=None):
    count = len(pieces)
    _, rows, width = pieces[0].shape
    rest = [] if out is None else [out]
    return pl.pallas_call(
        functools.partial(join_outputs_kernel, count, chosen),
        out_shape=jax.ShapeDtypeStruct((rows, width * count), pieces[0].dtype),
        in_specs=[SMEM] + [VMEM] * len(chosen) + [HBM] * len(rest),
        out_specs=HBM,
        scratch_shapes=[pltpu.SemaphoreType.DMA((count,))],
        input_output_aliases={1 + len(chosen): 0} if rest else {},
        compiler_params=room(6),
        cost_estimate=cost(0, 4 * rows * width * len(chosen)),
    )(places, *[pieces[i] for i in chosen], *rest)


def pack_kernel(chunks, ahead, wanted_ref, k_ref, v_ref, out_ref, buf, in_sem, out_sem):
    span, capacity = out_ref.shape[0] // chunks, wanted_ref.shape[2]

    def fetch(chunk):
        for i in range(chunk * span, (chunk + 1) * span):
            rows = pl.ds(pl.multiple_of(wanted_ref[i // capacity, 0, i % capacity] * BLK, BLK), BLK)
            pltpu.make_async_copy(k_ref.at[rows], buf.at[i, 0], in_sem.at[chunk]).start()
            pltpu.make_async_copy(v_ref.at[rows], buf.at[i, 1], in_sem.at[chunk]).start()

    copies = []
    for chunk in range(min(ahead, chunks)):
        fetch(chunk)
    for chunk in range(chunks):
        part = pl.ds(chunk * span, span)
        wait_for(buf.at[part], in_sem.at[chunk])
        copies.append(pltpu.make_async_copy(buf.at[part], out_ref.at[part], out_sem.at[chunk]))
        copies[-1].start()
        if chunk + ahead < chunks:
            fetch(chunk + ahead)
    for copy in copies:
        copy.wait()


def pack(wanted, keys, values, chunks=4, ahead=4):
    count = wanted.shape[0] * wanted.shape[2]
    return pl.pallas_call(
        functools.partial(pack_kernel, chunks, ahead),
        out_shape=jax.ShapeDtypeStruct((count, 2, BLK, HD), keys.dtype),
        in_specs=[SMEM, HBM, HBM],
        out_specs=HBM,
        scratch_shapes=[
            pltpu.VMEM((count, 2, BLK, HD), keys.dtype),
            pltpu.SemaphoreType.DMA((chunks,)),
            pltpu.SemaphoreType.DMA((chunks,)),
        ],
        cost_estimate=cost(0, 8 * count * BLK * HD),
    )(wanted, keys, values)


def scores_of(keys, queries):
    return lax.dot_general(keys, queries, (((1,), (1,)), ((), ())), preferred_element_type=jnp.float32)


def weighted(values, weights):
    return lax.dot_general(values, weights, (((0,), (0,)), ((), ())), preferred_element_type=jnp.float32)


def near_kernel(first, ids_ref, core_ref, qa_ref, qb_ref, k_ref, v_ref, kept_out, q_out, q_buf, k_buf, v_buf, kept_ref, q_ref, k_sem, v_sem, out_sem):
    blocks, picks, half = q_ref.shape[0], k_buf.shape[1] // BLK, qa_ref.shape[0]
    ratio = q_buf.shape[1] // HD
    factor = HD ** (-0.5) * LOG2E
    core = core_ref[0]
    for i in range(blocks):
        for j in range(picks):
            held = pl.ds(pl.multiple_of(ids_ref[first + i, j] * BLK, BLK), BLK)
            pltpu.make_async_copy(k_ref.at[held], k_buf.at[i, pl.ds(j * BLK, BLK)], k_sem.at[i]).start()
            pltpu.make_async_copy(v_ref.at[held], v_buf.at[i, pl.ds(j * BLK, BLK)], v_sem.at[i]).start()
    q_buf[pl.ds(pl.multiple_of(core * half, half), half), :] = qa_ref[...]
    q_buf[pl.ds(pl.multiple_of((1 - core) * half, half), half), :] = qb_ref[...]
    for i in range(blocks):
        for r in range(ratio):
            q_ref[i, r * BLK : (r + 1) * BLK, :] = q_buf[i * BLK : (i + 1) * BLK, r * HD : (r + 1) * HD]
    q_copy = pltpu.make_async_copy(q_ref, q_out, out_sem.at[0])
    q_copy.start()

    def block(i, carry):
        wait_for(k_buf.at[i], k_sem.at[i])
        wait_for(v_buf.at[i], v_sem.at[i])
        score = scores_of(k_buf[i], q_ref[i])
        highest = jnp.max(score, axis=0, keepdims=True) * factor
        exponent = jnp.exp2(score * factor - highest)
        kept_ref[i, HIGHEST : HIGHEST + 1, :] = highest
        kept_ref[i, TOTAL : TOTAL + 1, :] = jnp.sum(exponent, axis=0, keepdims=True)
        kept_ref[i, 0:HD, :] = weighted(v_buf[i], exponent.astype(jnp.bfloat16))
        return carry

    lax.fori_loop(0, blocks, block, 0)
    kept_copy = pltpu.make_async_copy(kept_ref, kept_out, out_sem.at[1])
    kept_copy.start()
    q_copy.wait()
    kept_copy.wait()


def near_attention(ids, first, core, qa, qb, keys, values):
    picks = ids.shape[1]
    rows, width = 2 * qa.shape[0], qa.shape[1]
    blocks = rows // BLK
    span, wide = picks * BLK, BLK * (width // HD)
    work = rows * width * span
    kept = [((blocks, KEPT_ROWS, wide), jnp.float32), ((blocks, wide, HD), qa.dtype)]
    return pl.pallas_call(
        functools.partial(near_kernel, first),
        out_shape=[jax.ShapeDtypeStruct(*what) for what in kept],
        in_specs=[SMEM, SMEM, VMEM, VMEM, HBM, HBM],
        out_specs=[HBM] * 2,
        scratch_shapes=[
            pltpu.VMEM((rows, width), qa.dtype),
            pltpu.VMEM((blocks, span, HD), keys.dtype),
            pltpu.VMEM((blocks, span, HD), keys.dtype),
            *[pltpu.VMEM(*what) for what in kept],
            pltpu.SemaphoreType.DMA((blocks,)),
            pltpu.SemaphoreType.DMA((blocks,)),
            pltpu.SemaphoreType.DMA((2,)),
        ],
        cost_estimate=cost(4 * work, 8 * rows * width + 4 * blocks * span * HD, work // HD),
    )(ids, core, qa, qb, keys, values)


def far_kernel(firsts, slots_ref, core_ref, got_ref, *refs):
    groups = len(firsts)
    near_refs, o_refs = refs[: 2 * groups], refs[2 * groups : 3 * groups]
    far_buf, far_sem = refs[3 * groups :]
    picks, half = far_buf.shape[1], o_refs[0].shape[1]
    ratio, blocks = o_refs[0].shape[2] // HD, far_buf.shape[0] // groups
    factor = HD ** (-0.5) * LOG2E
    core = core_ref[0]
    for n in range(groups * blocks):
        g, i = divmod(n, blocks)
        for j in range(picks):
            pltpu.make_async_copy(got_ref.at[slots_ref[firsts[g] + i, j]], far_buf.at[n, j], far_sem.at[n]).start()
    for n in range(groups * blocks):
        g, i = divmod(n, blocks)
        kept_ref, q_ref = near_refs[2 * g : 2 * g + 2]
        wait_for(far_buf.at[n], far_sem.at[n])
        keys = jnp.concatenate([far_buf[n, j, 0] for j in range(picks)], axis=0)
        values = jnp.concatenate([far_buf[n, j, 1] for j in range(picks)], axis=0)
        for r in range(ratio):
            queries = slice(r * BLK, (r + 1) * BLK)
            score = scores_of(keys, q_ref[i, queries, :])
            before = kept_ref[i, HIGHEST : HIGHEST + 1, queries]
            highest = jnp.maximum(jnp.max(score, axis=0, keepdims=True) * factor, before)
            exponent = jnp.exp2(score * factor - highest)
            kept = jnp.exp2(before - highest)
            total = jnp.sum(exponent, axis=0, keepdims=True) + kept * kept_ref[i, TOTAL : TOTAL + 1, queries]
            partial = weighted(values, exponent.astype(jnp.bfloat16))
            merged = (partial + kept * kept_ref[i, 0:HD, queries]) * (1.0 / total)
            turned = merged.T.astype(o_refs[g].dtype)
            for part in range(CORES):
                low, high = max(i * BLK, part * half), min((i + 1) * BLK, (part + 1) * half)
                if low < high:
                    place = core if part == 0 else 1 - core
                    rows = slice(low - part * half, high - part * half)
                    o_refs[g][place, rows, r * HD : (r + 1) * HD] = turned[low - i * BLK : high - i * BLK]


def far_attention(slots, firsts, core, got, near):
    groups, picks = len(firsts), slots.shape[1]
    _, q = near[0]
    blocks, wide = q.shape[0], q.shape[1]
    count = groups * blocks
    half, width = blocks * BLK // CORES, wide // BLK * HD
    return pl.pallas_call(
        functools.partial(far_kernel, firsts),
        out_shape=[jax.ShapeDtypeStruct((CORES, half, width), q.dtype)] * groups,
        in_specs=[SMEM, SMEM, HBM] + [VMEM] * (2 * groups),
        out_specs=[VMEM] * groups,
        scratch_shapes=[pltpu.VMEM((count, picks) + got.shape[1:], got.dtype), pltpu.SemaphoreType.DMA((count,))],
        compiler_params=room(16),
        cost_estimate=cost(1, 1),
    )(slots, core, got, *[array for group in near for array in group])


def offset_pairs(chips, chip_step, core_step):
    return [
        (chip * CORES + core, (chip + chip_step) % chips * CORES + (core ^ core_step))
        for chip in range(chips)
        for core in range(CORES)
    ]


def shards(queries, cache_keys, cache_values, block_ids):
    seq_count = lax.axis_size("seq")
    heads = lax.axis_size("head")
    seq_place = lax.axis_index("seq")
    head_place = lax.axis_index("head")
    chips = heads // CORES
    chip, core = head_place // CORES, head_place % CORES
    q_count, k_count = block_ids.shape[0], cache_keys.shape[0] // BLK
    per_chip = q_count // chips
    far_count = block_ids.shape[1] - NEAR
    capacity = max(2, (far_count * q_count + seq_count - 2) // (seq_count - 1))
    slot_total = seq_count * capacity

    far_ids = block_ids[:, NEAR:].reshape(-1)
    far_owner = far_ids // k_count
    far_within = far_ids - far_owner * k_count
    entry = jnp.arange(far_ids.shape[0], dtype=jnp.int32)
    earlier = (far_owner[:, None] == far_owner[None, :]) & (entry[None, :] < entry[:, None])
    far_slot = far_owner * capacity + jnp.sum(earlier.astype(jnp.int32), axis=1)
    slot_range = jnp.arange(slot_total, dtype=jnp.int32)
    unasked = slot_range % k_count
    placed = far_slot[:, None] == slot_range[None, :]
    asked = unasked + jnp.sum(jnp.where(placed, far_within[:, None] - unasked[None, :], 0), axis=0)
    wanted = lax.all_to_all(asked.reshape(seq_count, 1, capacity), "seq", split_axis=0, concat_axis=0, tiled=True)

    sent = pack(wanted, cache_keys, cache_values)
    got = lax.all_to_all(
        sent.reshape(seq_count, capacity, 2, BLK, HD), "seq", split_axis=0, concat_axis=0, tiled=True
    ).reshape(slot_total, 2, BLK, HD)

    steps = [(d, e) for d in range(chips) for e in range(CORES)]
    step_chip = jnp.array([d for d, _ in steps], jnp.int32)
    step_core = jnp.array([e for _, e in steps], jnp.int32)
    ahead = (chip + step_chip) % chips * CORES + (core + step_core) % CORES
    pieces = split_queries(queries, ahead)
    rows_of = {}
    for piece, (d, e) in zip(pieces, steps):
        rows_of[d, e] = piece if d == e == 0 else lax.ppermute(piece, "head", offset_pairs(chips, d, e))

    order = (chip - jnp.arange(chips, dtype=jnp.int32)) % chips
    own_ids = jnp.concatenate([block_ids[:, :NEAR] - seq_place * k_count, far_slot.reshape(q_count, far_count)], axis=1)
    own_ids = jnp.take(own_ids.reshape(chips, per_chip, -1), order, axis=0).reshape(q_count, -1)
    near_ids, slots = own_ids[:, :NEAR], own_ids[:, NEAR:]
    core_operand = core.astype(jnp.int32).reshape(1)
    near = [
        near_attention(near_ids, d * per_chip, core_operand, rows_of[d, 0], rows_of[d, 1], cache_keys, cache_values)
        for d in range(chips)
    ]
    got, near, slots = lax.optimization_barrier((got, near, slots))

    results = [None] * chips
    distance = lambda d: min(d, chips - d)
    for hops in range(chips // 2, -1, -1):
        group = [d for d in range(chips) if distance(d) == hops]
        if not hops:
            got, results[chips // 2] = lax.optimization_barrier((got, results[chips // 2]))
        made = far_attention(slots, tuple(d * per_chip for d in group), core_operand, got, [near[d] for d in group])
        if hops:
            made, got = lax.optimization_barrier((made, got))
        for d, rows in zip(group, made):
            results[d] = lax.ppermute(rows, "head", offset_pairs(chips, -d, 0)) if d else rows
    joined = []
    for d in range(chips):
        joined += [results[d], lax.ppermute(results[d], "head", offset_pairs(chips, 0, 1))]
    early = tuple(i for i in range(heads) if i // CORES in (0, chips // 2))
    late = tuple(i for i in range(heads) if i not in early)
    return join_outputs(joined, late, ahead, join_outputs(joined, early, ahead))


def solution(mesh):
    return jax.shard_map(
        shards,
        mesh=mesh,
        in_specs=(P(("seq", "head"), None), P("seq", "head"), P("seq", "head"), P("seq", None)),
        out_specs=P(("seq", "head"), None),
        check_vma=False,
    )
```

```python
import functools

import jax
import jax.numpy as jnp
from jax import lax
from jax.experimental import pallas as pl
from jax.experimental.pallas import tpu as pltpu
from jax.sharding import PartitionSpec as P

HD = 128
BLK = 128
NEAR = 5
CORES = 2
HBM = pl.BlockSpec(memory_space=pltpu.HBM)
SMEM = pl.BlockSpec(memory_space=pltpu.SMEM)
VMEM = pl.BlockSpec(memory_space=pltpu.VMEM)
LOG2E = 1.4426950408889634
HIGHEST, TOTAL, KEPT_ROWS = HD, HD + 1, HD + 8


def wait_for(ref, sem):
    pltpu.make_async_copy(ref, ref, sem).wait()


def room(mebibytes):
    return pltpu.CompilerParams(vmem_limit_bytes=mebibytes * 1024 * 1024)


def cost(flops, bytes_accessed, transcendentals=0):
    return pl.CostEstimate(flops=flops, bytes_accessed=bytes_accessed, transcendentals=transcendentals)


def split_queries_kernel(places_ref, q_ref, *refs):
    count = len(refs) - 3
    outs, buf, in_sem, out_sem = refs[:count], *refs[count:]
    width = buf.shape[2]
    into, out_of = [], []
    for i in range(count):
        start = pl.multiple_of(places_ref[i] * width, width)
        into.append(pltpu.make_async_copy(q_ref.at[:, pl.ds(start, width)], buf.at[i], in_sem.at[i]))
        out_of.append(pltpu.make_async_copy(buf.at[i], outs[i], out_sem.at[i]))
    for copy in into:
        copy.start()
    for i in range(count):
        into[i].wait()
        out_of[i].start()
    for copy in out_of:
        copy.wait()


def split_queries(queries, places):
    count = places.shape[0]
    rows, width = queries.shape[0], queries.shape[1] // count
    return pl.pallas_call(
        split_queries_kernel,
        out_shape=[jax.ShapeDtypeStruct((rows, width), queries.dtype)] * count,
        in_specs=[SMEM, HBM],
        out_specs=[HBM] * count,
        scratch_shapes=[
            pltpu.VMEM((count, rows, width), queries.dtype),
            pltpu.SemaphoreType.DMA((count,)),
            pltpu.SemaphoreType.DMA((count,)),
        ],
        cost_estimate=cost(0, 4 * queries.size),
    )(places, queries)


def join_outputs_kernel(count, chosen, places_ref, *refs):
    pieces, out_ref, sem = refs[: len(chosen)], refs[-2], refs[-1]
    width = out_ref.shape[1] // count
    copies = []
    for piece, i in zip(pieces, chosen):
        piece = piece.at[i % CORES] if len(piece.shape) == 3 else piece
        start = pl.multiple_of(places_ref[i] * width, width)
        copies.append(pltpu.make_async_copy(piece, out_ref.at[:, pl.ds(start, width)], sem.at[i]))
    for copy in copies:
        copy.start()
    for copy in copies:
        copy.wait()


def join_outputs(pieces, chosen, places, out=None):
    count = len(pieces)
    rows, width = pieces[0].shape[-2:]
    rest = [] if out is None else [out]
    return pl.pallas_call(
        functools.partial(join_outputs_kernel, count, chosen),
        out_shape=jax.ShapeDtypeStruct((rows, width * count), pieces[0].dtype),
        in_specs=[SMEM] + [VMEM] * len(chosen) + [HBM] * len(rest),
        out_specs=HBM,
        scratch_shapes=[pltpu.SemaphoreType.DMA((count,))],
        input_output_aliases={1 + len(chosen): 0} if rest else {},
        compiler_params=room(6),
        cost_estimate=cost(0, 4 * rows * width * len(chosen)),
    )(places, *[pieces[i] for i in chosen], *rest)


def pack_kernel(chunks, ahead, wanted_ref, k_ref, v_ref, out_ref, buf, in_sem, out_sem):
    span, capacity = out_ref.shape[0] // chunks, wanted_ref.shape[2]

    def fetch(chunk):
        for i in range(chunk * span, (chunk + 1) * span):
            rows = pl.ds(pl.multiple_of(wanted_ref[i // capacity, 0, i % capacity] * BLK, BLK), BLK)
            pltpu.make_async_copy(k_ref.at[rows], buf.at[i, 0], in_sem.at[chunk]).start()
            pltpu.make_async_copy(v_ref.at[rows], buf.at[i, 1], in_sem.at[chunk]).start()

    copies = []
    for chunk in range(min(ahead, chunks)):
        fetch(chunk)
    for chunk in range(chunks):
        part = pl.ds(chunk * span, span)
        wait_for(buf.at[part], in_sem.at[chunk])
        copies.append(pltpu.make_async_copy(buf.at[part], out_ref.at[part], out_sem.at[chunk]))
        copies[-1].start()
        if chunk + ahead < chunks:
            fetch(chunk + ahead)
    for copy in copies:
        copy.wait()


def pack(wanted, keys, values, chunks=4, ahead=4):
    count = wanted.shape[0] * wanted.shape[2]
    return pl.pallas_call(
        functools.partial(pack_kernel, chunks, ahead),
        out_shape=jax.ShapeDtypeStruct((count, 2, BLK, HD), keys.dtype),
        in_specs=[SMEM, HBM, HBM],
        out_specs=HBM,
        scratch_shapes=[
            pltpu.VMEM((count, 2, BLK, HD), keys.dtype),
            pltpu.SemaphoreType.DMA((chunks,)),
            pltpu.SemaphoreType.DMA((chunks,)),
        ],
        cost_estimate=cost(0, 8 * count * BLK * HD),
    )(wanted, keys, values)


def scores_of(keys, queries):
    return lax.dot_general(keys, queries, (((1,), (1,)), ((), ())), preferred_element_type=jnp.float32)


def weighted(values, weights):
    return lax.dot_general(values, weights, (((0,), (0,)), ((), ())), preferred_element_type=jnp.float32)


def near_kernel(first, ids_ref, core_ref, qa_ref, qb_ref, k_ref, v_ref, kept_out, q_out, q_buf, k_buf, v_buf, kept_ref, q_ref, k_sem, v_sem, out_sem):
    blocks, picks, half = q_ref.shape[0], k_buf.shape[1] // BLK, qa_ref.shape[0]
    ratio = q_buf.shape[1] // HD
    factor = HD ** (-0.5) * LOG2E
    core = core_ref[0]
    for i in range(blocks):
        for j in range(picks):
            held = pl.ds(pl.multiple_of(ids_ref[first + i, j] * BLK, BLK), BLK)
            pltpu.make_async_copy(k_ref.at[held], k_buf.at[i, pl.ds(j * BLK, BLK)], k_sem.at[i]).start()
            pltpu.make_async_copy(v_ref.at[held], v_buf.at[i, pl.ds(j * BLK, BLK)], v_sem.at[i]).start()
    q_buf[pl.ds(pl.multiple_of(core * half, half), half), :] = qa_ref[...]
    q_buf[pl.ds(pl.multiple_of((1 - core) * half, half), half), :] = qb_ref[...]
    for i in range(blocks):
        for r in range(ratio):
            q_ref[i, r * BLK : (r + 1) * BLK, :] = q_buf[i * BLK : (i + 1) * BLK, r * HD : (r + 1) * HD]
    q_copy = pltpu.make_async_copy(q_ref, q_out, out_sem.at[0])
    q_copy.start()

    def block(i, carry):
        wait_for(k_buf.at[i], k_sem.at[i])
        wait_for(v_buf.at[i], v_sem.at[i])
        score = scores_of(k_buf[i], q_ref[i])
        highest = jnp.max(score, axis=0, keepdims=True) * factor
        exponent = jnp.exp2(score * factor - highest)
        kept_ref[i, HIGHEST : HIGHEST + 1, :] = highest
        kept_ref[i, TOTAL : TOTAL + 1, :] = jnp.sum(exponent, axis=0, keepdims=True)
        kept_ref[i, 0:HD, :] = weighted(v_buf[i], exponent.astype(jnp.bfloat16))
        return carry

    lax.fori_loop(0, blocks, block, 0)
    kept_copy = pltpu.make_async_copy(kept_ref, kept_out, out_sem.at[1])
    kept_copy.start()
    q_copy.wait()
    kept_copy.wait()


def near_attention(ids, first, core, qa, qb, keys, values):
    picks = ids.shape[1]
    rows, width = 2 * qa.shape[0], qa.shape[1]
    blocks = rows // BLK
    span, wide = picks * BLK, BLK * (width // HD)
    work = rows * width * span
    kept = [((blocks, KEPT_ROWS, wide), jnp.float32), ((blocks, wide, HD), qa.dtype)]
    return pl.pallas_call(
        functools.partial(near_kernel, first),
        out_shape=[jax.ShapeDtypeStruct(*what) for what in kept],
        in_specs=[SMEM, SMEM, VMEM, VMEM, HBM, HBM],
        out_specs=[HBM] * 2,
        scratch_shapes=[
            pltpu.VMEM((rows, width), qa.dtype),
            pltpu.VMEM((blocks, span, HD), keys.dtype),
            pltpu.VMEM((blocks, span, HD), keys.dtype),
            *[pltpu.VMEM(*what) for what in kept],
            pltpu.SemaphoreType.DMA((blocks,)),
            pltpu.SemaphoreType.DMA((blocks,)),
            pltpu.SemaphoreType.DMA((2,)),
        ],
        cost_estimate=cost(4 * work, 8 * rows * width + 4 * blocks * span * HD, work // HD),
    )(ids, core, qa, qb, keys, values)


def far_kernel(firsts, split, slots_ref, core_ref, got_ref, *refs):
    groups = len(firsts)
    near_refs, o_refs, far_buf, o_buf, far_sem = refs[: 2 * groups], refs[2 * groups : -3], *refs[-3:]
    picks, half = far_buf.shape[1], o_buf.shape[2]
    ratio, blocks = o_buf.shape[3] // HD, far_buf.shape[0] // groups
    factor = HD ** (-0.5) * LOG2E
    core = core_ref[0]
    for n in range(groups * blocks):
        g, i = divmod(n, blocks)
        for j in range(picks):
            pltpu.make_async_copy(got_ref.at[slots_ref[firsts[g] + i, j]], far_buf.at[n, j], far_sem).start()
    wait_for(far_buf, far_sem)
    for n in range(groups * blocks):
        g, i = divmod(n, blocks)
        kept_ref, q_ref = near_refs[2 * g : 2 * g + 2]
        keys = jnp.concatenate([far_buf[n, j, 0] for j in range(picks)], axis=0)
        values = jnp.concatenate([far_buf[n, j, 1] for j in range(picks)], axis=0)
        for r in range(ratio):
            queries = slice(r * BLK, (r + 1) * BLK)
            score = scores_of(keys, q_ref[i, queries, :])
            before = kept_ref[i, HIGHEST : HIGHEST + 1, queries]
            highest = jnp.maximum(jnp.max(score, axis=0, keepdims=True) * factor, before)
            exponent = jnp.exp2(score * factor - highest)
            kept = jnp.exp2(before - highest)
            total = jnp.sum(exponent, axis=0, keepdims=True) + kept * kept_ref[i, TOTAL : TOTAL + 1, queries]
            partial = weighted(values, exponent.astype(jnp.bfloat16))
            merged = (partial + kept * kept_ref[i, 0:HD, queries]) * (1.0 / total)
            turned = merged.T.astype(o_buf.dtype)
            for part in range(CORES):
                low, high = max(i * BLK, part * half), min((i + 1) * BLK, (part + 1) * half)
                if low < high:
                    rows = slice(low - part * half, high - part * half)
                    o_buf[g, part, rows, r * HD : (r + 1) * HD] = turned[low - i * BLK : high - i * BLK]
    for g in range(groups):
        for part in range(CORES):
            if split:
                o_refs[CORES * g + part][...] = o_buf[g, core if part == 0 else 1 - core]
            else:
                o_refs[g][core if part == 0 else 1 - core] = o_buf[g, part]


def far_attention(slots, firsts, split, core, got, near):
    groups, picks = len(firsts), slots.shape[1]
    _, q = near[0]
    blocks, wide = q.shape[0], q.shape[1]
    count = groups * blocks
    half, width = blocks * BLK // CORES, wide // BLK * HD
    out_shape = [jax.ShapeDtypeStruct((CORES, half, width), q.dtype)] * groups
    if split:
        out_shape = [jax.ShapeDtypeStruct((half, width), q.dtype)] * (CORES * groups)
    return pl.pallas_call(
        functools.partial(far_kernel, firsts, split),
        out_shape=out_shape,
        in_specs=[SMEM, SMEM, HBM] + [VMEM] * (2 * groups),
        out_specs=[VMEM] * len(out_shape),
        scratch_shapes=[
            pltpu.VMEM((count, picks) + got.shape[1:], got.dtype),
            pltpu.VMEM((groups, CORES, half, width), q.dtype),
            pltpu.SemaphoreType.DMA,
        ],
        compiler_params=room(16),
        cost_estimate=cost(1, 1),
    )(slots, core, got, *[array for group in near for array in group])


def offset_pairs(chips, chip_step, core_step):
    return [
        (chip * CORES + core, (chip + chip_step) % chips * CORES + (core ^ core_step))
        for chip in range(chips)
        for core in range(CORES)
    ]


def shards(queries, cache_keys, cache_values, block_ids):
    seq_count = lax.axis_size("seq")
    heads = lax.axis_size("head")
    seq_place = lax.axis_index("seq")
    head_place = lax.axis_index("head")
    chips = heads // CORES
    chip, core = head_place // CORES, head_place % CORES
    q_count, k_count = block_ids.shape[0], cache_keys.shape[0] // BLK
    per_chip = q_count // chips
    far_count = block_ids.shape[1] - NEAR
    capacity = max(2, (far_count * q_count + seq_count - 2) // (seq_count - 1))
    slot_total = seq_count * capacity

    far_ids = block_ids[:, NEAR:].reshape(-1)
    far_owner = far_ids // k_count
    far_within = far_ids - far_owner * k_count
    entry = jnp.arange(far_ids.shape[0], dtype=jnp.int32)
    earlier = (far_owner[:, None] == far_owner[None, :]) & (entry[None, :] < entry[:, None])
    far_slot = far_owner * capacity + jnp.sum(earlier.astype(jnp.int32), axis=1)
    slot_range = jnp.arange(slot_total, dtype=jnp.int32)
    unasked = slot_range % k_count
    placed = far_slot[:, None] == slot_range[None, :]
    asked = unasked + jnp.sum(jnp.where(placed, far_within[:, None] - unasked[None, :], 0), axis=0)
    wanted = lax.all_to_all(asked.reshape(seq_count, 1, capacity), "seq", split_axis=0, concat_axis=0, tiled=True)

    sent = pack(wanted, cache_keys, cache_values)
    got = lax.all_to_all(
        sent.reshape(seq_count, capacity, 2, BLK, HD), "seq", split_axis=0, concat_axis=0, tiled=True
    ).reshape(slot_total, 2, BLK, HD)

    steps = [(d, e) for d in range(chips) for e in range(CORES)]
    step_chip = jnp.array([d for d, _ in steps], jnp.int32)
    step_core = jnp.array([e for _, e in steps], jnp.int32)
    ahead = (chip + step_chip) % chips * CORES + (core + step_core) % CORES
    pieces = split_queries(queries, ahead)
    rows_of = {}
    for piece, (d, e) in zip(pieces, steps):
        rows_of[d, e] = piece if d == e == 0 else lax.ppermute(piece, "head", offset_pairs(chips, d, e))

    order = (chip - jnp.arange(chips, dtype=jnp.int32)) % chips
    own_ids = jnp.concatenate([block_ids[:, :NEAR] - seq_place * k_count, far_slot.reshape(q_count, far_count)], axis=1)
    own_ids = jnp.take(own_ids.reshape(chips, per_chip, -1), order, axis=0).reshape(q_count, -1)
    near_ids, slots = own_ids[:, :NEAR], own_ids[:, NEAR:]
    core_operand = core.astype(jnp.int32).reshape(1)
    near = [
        near_attention(near_ids, d * per_chip, core_operand, rows_of[d, 0], rows_of[d, 1], cache_keys, cache_values)
        for d in range(chips)
    ]
    got, near, slots = lax.optimization_barrier((got, near, slots))

    joined = [None] * heads

    def attend(group, split, got):
        return far_attention(slots, tuple(d * per_chip for d in group), split, core_operand, got, [near[d] for d in group])

    def send(rows, d, e):
        return lax.ppermute(rows, "head", offset_pairs(chips, -d, e))

    far_chip = chips // 2
    made, got = lax.optimization_barrier((attend([far_chip], False, got), got))
    farthest = send(made[0], far_chip, 0)
    between = [d for d in range(1, chips) if d != far_chip]
    made = attend(between + [0], True, got)
    late = []
    for e in range(CORES):
        for n, d in enumerate(between):
            joined[CORES * d + e] = send(made[CORES * n + e], d, e)
            late.append(CORES * d + e)
    joined[CORES * far_chip : CORES * (far_chip + 1)] = [farthest, send(farthest, 0, 1)]
    joined[:CORES] = [made[-CORES], send(made[-1], 0, 1)]
    early = [i for i in range(heads) if i not in late]
    return join_outputs(joined, tuple(late + early), ahead)


def solution(mesh):
    return jax.shard_map(
        shards,
        mesh=mesh,
        in_specs=(P(("seq", "head"), None), P("seq", "head"), P("seq", "head"), P("seq", None)),
        out_specs=P(("seq", "head"), None),
        check_vma=False,
    )
```

```python
import functools

import jax
import jax.numpy as jnp
from jax import lax
from jax.experimental import pallas as pl
from jax.experimental.pallas import tpu as pltpu
from jax.sharding import PartitionSpec as P

HD = 128
BLK = 128
NEAR = 5
CORES = 2
HBM = pl.BlockSpec(memory_space=pltpu.HBM)
SMEM = pl.BlockSpec(memory_space=pltpu.SMEM)
VMEM = pl.BlockSpec(memory_space=pltpu.VMEM)
LOG2E = 1.4426950408889634
HIGHEST, TOTAL, KEPT_ROWS = HD, HD + 1, HD + 8


def wait_for(ref, sem):
    pltpu.make_async_copy(ref, ref, sem).wait()


def room(mebibytes):
    return pltpu.CompilerParams(vmem_limit_bytes=mebibytes * 1024 * 1024)


def cost(flops, bytes_accessed, transcendentals=0):
    return pl.CostEstimate(flops=flops, bytes_accessed=bytes_accessed, transcendentals=transcendentals)


def split_queries_kernel(places_ref, q_ref, *refs):
    count = len(refs) - 3
    outs, buf, in_sem, out_sem = refs[:count], *refs[count:]
    width = buf.shape[2]
    into, out_of = [], []
    for i in range(count):
        start = pl.multiple_of(places_ref[i] * width, width)
        into.append(pltpu.make_async_copy(q_ref.at[:, pl.ds(start, width)], buf.at[i], in_sem.at[i]))
        out_of.append(pltpu.make_async_copy(buf.at[i], outs[i], out_sem.at[i]))
    for copy in into:
        copy.start()
    for i in range(count):
        into[i].wait()
        out_of[i].start()
    for copy in out_of:
        copy.wait()


def split_queries(queries, places):
    count = places.shape[0]
    rows, width = queries.shape[0], queries.shape[1] // count
    return pl.pallas_call(
        split_queries_kernel,
        out_shape=[jax.ShapeDtypeStruct((rows, width), queries.dtype)] * count,
        in_specs=[SMEM, HBM],
        out_specs=[HBM] * count,
        scratch_shapes=[
            pltpu.VMEM((count, rows, width), queries.dtype),
            pltpu.SemaphoreType.DMA((count,)),
            pltpu.SemaphoreType.DMA((count,)),
        ],
        cost_estimate=cost(0, 4 * queries.size),
    )(places, queries)


def join_outputs_kernel(count, chosen, places_ref, *refs):
    pieces, out_ref, sem = refs[: len(chosen)], refs[-2], refs[-1]
    width = out_ref.shape[1] // count
    copies = []
    for piece, i in zip(pieces, chosen):
        start = pl.multiple_of(places_ref[i] * width, width)
        copies.append(pltpu.make_async_copy(piece.at[i % CORES], out_ref.at[:, pl.ds(start, width)], sem.at[i]))
    for copy in copies:
        copy.start()
    for copy in copies:
        copy.wait()


def join_outputs(pieces, chosen, places, out=None):
    count = len(pieces)
    _, rows, width = pieces[0].shape
    rest = [] if out is None else [out]
    return pl.pallas_call(
        functools.partial(join_outputs_kernel, count, chosen),
        out_shape=jax.ShapeDtypeStruct((rows, width * count), pieces[0].dtype),
        in_specs=[SMEM] + [VMEM] * len(chosen) + [HBM] * len(rest),
        out_specs=HBM,
        scratch_shapes=[pltpu.SemaphoreType.DMA((count,))],
        input_output_aliases={1 + len(chosen): 0} if rest else {},
        compiler_params=room(6),
        cost_estimate=cost(0, 4 * rows * width * len(chosen)),
    )(places, *[pieces[i] for i in chosen], *rest)


def pack_kernel(chunks, unroll, wanted_ref, k_ref, v_ref, out_ref, buf, in_sem, out_sem):
    span, capacity = out_ref.shape[0] // chunks, wanted_ref.shape[2]
    owners = span // capacity
    copies = []
    for chunk in range(chunks):

        def fetch(owner, carry):
            for j in range(capacity):
                rows = pl.ds(pl.multiple_of(wanted_ref[owner, 0, j] * BLK, BLK), BLK)
                place = owner * capacity + j
                pltpu.make_async_copy(k_ref.at[rows], buf.at[place, 0], in_sem.at[chunk]).start()
                pltpu.make_async_copy(v_ref.at[rows], buf.at[place, 1], in_sem.at[chunk]).start()
            return carry

        lax.fori_loop(chunk * owners, (chunk + 1) * owners, fetch, 0, unroll=unroll)
    for chunk in range(chunks):
        part = pl.ds(chunk * span, span)
        wait_for(buf.at[part], in_sem.at[chunk])
        copies.append(pltpu.make_async_copy(buf.at[part], out_ref.at[part], out_sem.at[chunk]))
        copies[-1].start()
    for copy in copies:
        copy.wait()


def pack(wanted, keys, values, chunks=4, unroll=2):
    count = wanted.shape[0] * wanted.shape[2]
    return pl.pallas_call(
        functools.partial(pack_kernel, chunks, unroll),
        out_shape=jax.ShapeDtypeStruct((count, 2, BLK, HD), keys.dtype),
        in_specs=[SMEM, HBM, HBM],
        out_specs=HBM,
        scratch_shapes=[
            pltpu.VMEM((count, 2, BLK, HD), keys.dtype),
            pltpu.SemaphoreType.DMA((chunks,)),
            pltpu.SemaphoreType.DMA((chunks,)),
        ],
        cost_estimate=cost(0, 8 * count * BLK * HD),
    )(wanted, keys, values)


def scores_of(keys, queries):
    return lax.dot_general(keys, queries, (((1,), (1,)), ((), ())), preferred_element_type=jnp.float32)


def weighted(values, weights):
    return lax.dot_general(values, weights, (((0,), (0,)), ((), ())), preferred_element_type=jnp.float32)


def near_kernel(first, ids_ref, core_ref, qa_ref, qb_ref, k_ref, v_ref, kept_out, q_out, q_buf, k_buf, v_buf, kept_ref, q_ref, k_sem, v_sem, out_sem):
    blocks, picks, half = q_ref.shape[0], k_buf.shape[1] // BLK, qa_ref.shape[0]
    ratio = q_buf.shape[1] // HD
    factor = HD ** (-0.5) * LOG2E
    core = core_ref[0]
    for i in range(blocks):
        for j in range(picks):
            held = pl.ds(pl.multiple_of(ids_ref[first + i, j] * BLK, BLK), BLK)
            pltpu.make_async_copy(k_ref.at[held], k_buf.at[i, pl.ds(j * BLK, BLK)], k_sem.at[i]).start()
            pltpu.make_async_copy(v_ref.at[held], v_buf.at[i, pl.ds(j * BLK, BLK)], v_sem.at[i]).start()
    q_buf[pl.ds(pl.multiple_of(core * half, half), half), :] = qa_ref[...]
    q_buf[pl.ds(pl.multiple_of((1 - core) * half, half), half), :] = qb_ref[...]
    for i in range(blocks):
        for r in range(ratio):
            q_ref[i, r * BLK : (r + 1) * BLK, :] = q_buf[i * BLK : (i + 1) * BLK, r * HD : (r + 1) * HD]
    q_copy = pltpu.make_async_copy(q_ref, q_out, out_sem.at[0])
    q_copy.start()

    def block(i, carry):
        wait_for(k_buf.at[i], k_sem.at[i])
        wait_for(v_buf.at[i], v_sem.at[i])
        score = scores_of(k_buf[i], q_ref[i])
        highest = jnp.max(score, axis=0, keepdims=True) * factor
        exponent = jnp.exp2(score * factor - highest)
        kept_ref[i, HIGHEST : HIGHEST + 1, :] = highest
        kept_ref[i, TOTAL : TOTAL + 1, :] = jnp.sum(exponent, axis=0, keepdims=True)
        kept_ref[i, 0:HD, :] = weighted(v_buf[i], exponent.astype(jnp.bfloat16))
        return carry

    lax.fori_loop(0, blocks, block, 0)
    kept_copy = pltpu.make_async_copy(kept_ref, kept_out, out_sem.at[1])
    kept_copy.start()
    q_copy.wait()
    kept_copy.wait()


def near_attention(ids, first, core, qa, qb, keys, values):
    picks = ids.shape[1]
    rows, width = 2 * qa.shape[0], qa.shape[1]
    blocks = rows // BLK
    span, wide = picks * BLK, BLK * (width // HD)
    work = rows * width * span
    kept = [((blocks, KEPT_ROWS, wide), jnp.float32), ((blocks, wide, HD), qa.dtype)]
    return pl.pallas_call(
        functools.partial(near_kernel, first),
        out_shape=[jax.ShapeDtypeStruct(*what) for what in kept],
        in_specs=[SMEM, SMEM, VMEM, VMEM, HBM, HBM],
        out_specs=[HBM] * 2,
        scratch_shapes=[
            pltpu.VMEM((rows, width), qa.dtype),
            pltpu.VMEM((blocks, span, HD), keys.dtype),
            pltpu.VMEM((blocks, span, HD), keys.dtype),
            *[pltpu.VMEM(*what) for what in kept],
            pltpu.SemaphoreType.DMA((blocks,)),
            pltpu.SemaphoreType.DMA((blocks,)),
            pltpu.SemaphoreType.DMA((2,)),
        ],
        cost_estimate=cost(4 * work, 8 * rows * width + 4 * blocks * span * HD, work // HD),
    )(ids, core, qa, qb, keys, values)


def far_kernel(firsts, slots_ref, core_ref, got_ref, *refs):
    groups = len(firsts)
    near_refs, o_refs = refs[: 2 * groups], refs[2 * groups : 3 * groups]
    far_buf, o_buf, far_sem = refs[3 * groups :]
    picks, half = far_buf.shape[1], o_buf.shape[2]
    ratio, blocks = o_buf.shape[3] // HD, far_buf.shape[0] // groups
    factor = HD ** (-0.5) * LOG2E
    core = core_ref[0]
    for n in range(groups * blocks):
        g, i = divmod(n, blocks)
        for j in range(picks):
            pltpu.make_async_copy(got_ref.at[slots_ref[firsts[g] + i, j]], far_buf.at[n, j], far_sem).start()
    wait_for(far_buf, far_sem)
    for n in range(groups * blocks):
        g, i = divmod(n, blocks)
        kept_ref, q_ref = near_refs[2 * g : 2 * g + 2]
        keys = jnp.concatenate([far_buf[n, j, 0] for j in range(picks)], axis=0)
        values = jnp.concatenate([far_buf[n, j, 1] for j in range(picks)], axis=0)
        for r in range(ratio):
            queries = slice(r * BLK, (r + 1) * BLK)
            score = scores_of(keys, q_ref[i, queries, :])
            before = kept_ref[i, HIGHEST : HIGHEST + 1, queries]
            highest = jnp.maximum(jnp.max(score, axis=0, keepdims=True) * factor, before)
            exponent = jnp.exp2(score * factor - highest)
            kept = jnp.exp2(before - highest)
            total = jnp.sum(exponent, axis=0, keepdims=True) + kept * kept_ref[i, TOTAL : TOTAL + 1, queries]
            partial = weighted(values, exponent.astype(jnp.bfloat16))
            merged = (partial + kept * kept_ref[i, 0:HD, queries]) * (1.0 / total)
            turned = merged.T.astype(o_buf.dtype)
            for part in range(CORES):
                low, high = max(i * BLK, part * half), min((i + 1) * BLK, (part + 1) * half)
                if low < high:
                    rows = slice(low - part * half, high - part * half)
                    o_buf[g, part, rows, r * HD : (r + 1) * HD] = turned[low - i * BLK : high - i * BLK]
    for g in range(groups):
        for part in range(CORES):
            o_refs[g][core if part == 0 else 1 - core] = o_buf[g, part]


def far_attention(slots, firsts, core, got, near):
    groups, picks = len(firsts), slots.shape[1]
    _, q = near[0]
    blocks, wide = q.shape[0], q.shape[1]
    count = groups * blocks
    half, width = blocks * BLK // CORES, wide // BLK * HD
    return pl.pallas_call(
        functools.partial(far_kernel, firsts),
        out_shape=[jax.ShapeDtypeStruct((CORES, half, width), q.dtype)] * groups,
        in_specs=[SMEM, SMEM, HBM] + [VMEM] * (2 * groups),
        out_specs=[VMEM] * groups,
        scratch_shapes=[
            pltpu.VMEM((count, picks) + got.shape[1:], got.dtype),
            pltpu.VMEM((groups, CORES, half, width), q.dtype),
            pltpu.SemaphoreType.DMA,
        ],
        compiler_params=room(16),
        cost_estimate=cost(1, 1),
    )(slots, core, got, *[array for group in near for array in group])


def offset_pairs(chips, chip_step, core_step):
    return [
        (chip * CORES + core, (chip + chip_step) % chips * CORES + (core ^ core_step))
        for chip in range(chips)
        for core in range(CORES)
    ]


def shards(queries, cache_keys, cache_values, block_ids):
    seq_count = lax.axis_size("seq")
    heads = lax.axis_size("head")
    seq_place = lax.axis_index("seq")
    head_place = lax.axis_index("head")
    chips = heads // CORES
    chip, core = head_place // CORES, head_place % CORES
    q_count, k_count = block_ids.shape[0], cache_keys.shape[0] // BLK
    per_chip = q_count // chips
    far_count = block_ids.shape[1] - NEAR
    capacity = max(2, (far_count * q_count + seq_count - 2) // (seq_count - 1))
    slot_total = seq_count * capacity

    far_ids = block_ids[:, NEAR:].reshape(-1)
    far_owner = far_ids // k_count
    far_within = far_ids - far_owner * k_count
    entry = jnp.arange(far_ids.shape[0], dtype=jnp.int32)
    earlier = (far_owner[:, None] == far_owner[None, :]) & (entry[None, :] < entry[:, None])
    far_slot = far_owner * capacity + jnp.sum(earlier.astype(jnp.int32), axis=1)
    slot_range = jnp.arange(slot_total, dtype=jnp.int32)
    unasked = slot_range % k_count
    placed = far_slot[:, None] == slot_range[None, :]
    asked = unasked + jnp.sum(jnp.where(placed, far_within[:, None] - unasked[None, :], 0), axis=0)
    wanted = lax.all_to_all(asked.reshape(seq_count, 1, capacity), "seq", split_axis=0, concat_axis=0, tiled=True)

    sent = pack(wanted, cache_keys, cache_values)
    got = lax.all_to_all(
        sent.reshape(seq_count, capacity, 2, BLK, HD), "seq", split_axis=0, concat_axis=0, tiled=True
    ).reshape(slot_total, 2, BLK, HD)

    steps = [(d, e) for d in range(chips) for e in range(CORES)]
    step_chip = jnp.array([d for d, _ in steps], jnp.int32)
    step_core = jnp.array([e for _, e in steps], jnp.int32)
    ahead = (chip + step_chip) % chips * CORES + (core + step_core) % CORES
    pieces = split_queries(queries, ahead)
    rows_of = {}
    for piece, (d, e) in zip(pieces, steps):
        rows_of[d, e] = piece if d == e == 0 else lax.ppermute(piece, "head", offset_pairs(chips, d, e))

    order = (chip - jnp.arange(chips, dtype=jnp.int32)) % chips
    own_ids = jnp.concatenate([block_ids[:, :NEAR] - seq_place * k_count, far_slot.reshape(q_count, far_count)], axis=1)
    own_ids = jnp.take(own_ids.reshape(chips, per_chip, -1), order, axis=0).reshape(q_count, -1)
    near_ids, slots = own_ids[:, :NEAR], own_ids[:, NEAR:]
    core_operand = core.astype(jnp.int32).reshape(1)
    near = [
        near_attention(near_ids, d * per_chip, core_operand, rows_of[d, 0], rows_of[d, 1], cache_keys, cache_values)
        for d in range(chips)
    ]
    got, near, slots = lax.optimization_barrier((got, near, slots))

    results = [None] * chips
    distance = lambda d: min(d, chips - d)
    for hops in range(chips // 2, -1, -1):
        group = [d for d in range(chips) if distance(d) == hops]
        if not hops:
            got, results[chips // 2] = lax.optimization_barrier((got, results[chips // 2]))
        made = far_attention(slots, tuple(d * per_chip for d in group), core_operand, got, [near[d] for d in group])
        if hops:
            made, got = lax.optimization_barrier((made, got))
        for d, rows in zip(group, made):
            results[d] = lax.ppermute(rows, "head", offset_pairs(chips, -d, 0)) if d else rows
    joined = []
    for d in range(chips):
        joined += [results[d], lax.ppermute(results[d], "head", offset_pairs(chips, 0, 1))]
    early = tuple(i for i in range(heads) if i // CORES in (0, chips // 2))
    late = tuple(i for i in range(heads) if i not in early)
    return join_outputs(joined, late, ahead, join_outputs(joined, early, ahead))


def solution(mesh):
    return jax.shard_map(
        shards,
        mesh=mesh,
        in_specs=(P(("seq", "head"), None), P("seq", "head"), P("seq", "head"), P("seq", None)),
        out_specs=P(("seq", "head"), None),
        check_vma=False,
    )
```

```python
import functools

import jax
import jax.numpy as jnp
from jax import lax
from jax.experimental import pallas as pl
from jax.experimental.pallas import tpu as pltpu
from jax.sharding import PartitionSpec as P

HD = 128
BLK = 128
NEAR = 5
CORES = 2
HBM = pl.BlockSpec(memory_space=pltpu.HBM)
SMEM = pl.BlockSpec(memory_space=pltpu.SMEM)
VMEM = pl.BlockSpec(memory_space=pltpu.VMEM)
LOG2E = 1.4426950408889634
HIGHEST, TOTAL, KEPT_ROWS = HD, HD + 1, HD + 8


def wait_for(ref, sem):
    pltpu.make_async_copy(ref, ref, sem).wait()


def room(mebibytes):
    return pltpu.CompilerParams(vmem_limit_bytes=mebibytes * 1024 * 1024)


def cost(flops, bytes_accessed, transcendentals=0):
    return pl.CostEstimate(flops=flops, bytes_accessed=bytes_accessed, transcendentals=transcendentals)


def split_queries_kernel(places_ref, q_ref, *refs):
    count = len(refs) - 3
    outs, buf, in_sem, out_sem = refs[:count], *refs[count:]
    width = buf.shape[2]
    into, out_of = [], []
    for i in range(count):
        start = pl.multiple_of(places_ref[i] * width, width)
        into.append(pltpu.make_async_copy(q_ref.at[:, pl.ds(start, width)], buf.at[i], in_sem.at[i]))
        out_of.append(pltpu.make_async_copy(buf.at[i], outs[i], out_sem.at[i]))
    for copy in into:
        copy.start()
    for i in range(count):
        into[i].wait()
        out_of[i].start()
    for copy in out_of:
        copy.wait()


def split_queries(queries, places):
    count = places.shape[0]
    rows, width = queries.shape[0], queries.shape[1] // count
    return pl.pallas_call(
        split_queries_kernel,
        out_shape=[jax.ShapeDtypeStruct((rows, width), queries.dtype)] * count,
        in_specs=[SMEM, HBM],
        out_specs=[HBM] * count,
        scratch_shapes=[
            pltpu.VMEM((count, rows, width), queries.dtype),
            pltpu.SemaphoreType.DMA((count,)),
            pltpu.SemaphoreType.DMA((count,)),
        ],
        cost_estimate=cost(0, 4 * queries.size),
    )(places, queries)


def join_outputs_kernel(count, chosen, places_ref, *refs):
    pieces, out_ref, sem = refs[: len(chosen)], refs[-2], refs[-1]
    width = out_ref.shape[1] // count
    copies = []
    for piece, i in zip(pieces, chosen):
        start = pl.multiple_of(places_ref[i] * width, width)
        copies.append(pltpu.make_async_copy(piece.at[i % CORES], out_ref.at[:, pl.ds(start, width)], sem.at[i]))
    for copy in copies:
        copy.start()
    for copy in copies:
        copy.wait()


def join_outputs(pieces, chosen, places, out=None):
    count = len(pieces)
    _, rows, width = pieces[0].shape
    rest = [] if out is None else [out]
    return pl.pallas_call(
        functools.partial(join_outputs_kernel, count, chosen),
        out_shape=jax.ShapeDtypeStruct((rows, width * count), pieces[0].dtype),
        in_specs=[SMEM] + [VMEM] * len(chosen) + [HBM] * len(rest),
        out_specs=HBM,
        scratch_shapes=[pltpu.SemaphoreType.DMA((count,))],
        input_output_aliases={1 + len(chosen): 0} if rest else {},
        compiler_params=room(6),
        cost_estimate=cost(0, 4 * rows * width * len(chosen)),
    )(places, *[pieces[i] for i in chosen], *rest)


def hold_kernel(k_ref, k_out, sem):
    copy = pltpu.make_async_copy(k_ref, k_out, sem)
    copy.start()
    copy.wait()


def hold(keys):
    return pl.pallas_call(
        hold_kernel,
        out_shape=jax.ShapeDtypeStruct(keys.shape, keys.dtype),
        in_specs=[HBM],
        out_specs=VMEM,
        scratch_shapes=[pltpu.SemaphoreType.DMA],
        compiler_params=room(6),
        cost_estimate=cost(0, 4 * keys.size),
    )(keys)


def pack_kernel(wanted_ref, k_ref, v_ref, out_ref):
    capacity = wanted_ref.shape[2]
    for place in range(out_ref.shape[0]):
        wanted = wanted_ref[place // capacity, 0, place % capacity]
        rows = pl.ds(pl.multiple_of(wanted * BLK, BLK), BLK)
        out_ref[place, 0] = k_ref[rows, :]
        out_ref[place, 1] = v_ref[rows, :]


def pack(wanted, keys, values):
    count = wanted.shape[0] * wanted.shape[2]
    return pl.pallas_call(
        pack_kernel,
        out_shape=jax.ShapeDtypeStruct((count, 2, BLK, HD), keys.dtype),
        in_specs=[SMEM, VMEM, VMEM],
        out_specs=VMEM,
        compiler_params=room(12),
        cost_estimate=cost(0, 8 * count * BLK * HD),
    )(wanted, keys, values)


def scores_of(keys, queries):
    return lax.dot_general(keys, queries, (((1,), (1,)), ((), ())), preferred_element_type=jnp.float32)


def weighted(values, weights):
    return lax.dot_general(values, weights, (((0,), (0,)), ((), ())), preferred_element_type=jnp.float32)


def near_kernel(first, ids_ref, core_ref, qa_ref, qb_ref, k_ref, v_ref, kept_out, q_out, q_buf, k_buf, v_buf, kept_ref, q_ref, k_sem, v_sem, out_sem):
    blocks, picks, half = q_ref.shape[0], k_buf.shape[1] // BLK, qa_ref.shape[0]
    ratio = q_buf.shape[1] // HD
    factor = HD ** (-0.5) * LOG2E
    core = core_ref[0]
    for i in range(blocks):
        for j in range(picks):
            held = pl.ds(pl.multiple_of(ids_ref[first + i, j] * BLK, BLK), BLK)
            pltpu.make_async_copy(k_ref.at[held], k_buf.at[i, pl.ds(j * BLK, BLK)], k_sem.at[i]).start()
            pltpu.make_async_copy(v_ref.at[held], v_buf.at[i, pl.ds(j * BLK, BLK)], v_sem.at[i]).start()
    q_buf[pl.ds(pl.multiple_of(core * half, half), half), :] = qa_ref[...]
    q_buf[pl.ds(pl.multiple_of((1 - core) * half, half), half), :] = qb_ref[...]
    for i in range(blocks):
        for r in range(ratio):
            q_ref[i, r * BLK : (r + 1) * BLK, :] = q_buf[i * BLK : (i + 1) * BLK, r * HD : (r + 1) * HD]
    q_copy = pltpu.make_async_copy(q_ref, q_out, out_sem.at[0])
    q_copy.start()

    def block(i, carry):
        wait_for(k_buf.at[i], k_sem.at[i])
        wait_for(v_buf.at[i], v_sem.at[i])
        score = scores_of(k_buf[i], q_ref[i])
        highest = jnp.max(score, axis=0, keepdims=True) * factor
        exponent = jnp.exp2(score * factor - highest)
        kept_ref[i, HIGHEST : HIGHEST + 1, :] = highest
        kept_ref[i, TOTAL : TOTAL + 1, :] = jnp.sum(exponent, axis=0, keepdims=True)
        kept_ref[i, 0:HD, :] = weighted(v_buf[i], exponent.astype(jnp.bfloat16))
        return carry

    lax.fori_loop(0, blocks, block, 0)
    kept_copy = pltpu.make_async_copy(kept_ref, kept_out, out_sem.at[1])
    kept_copy.start()
    q_copy.wait()
    kept_copy.wait()


def near_attention(ids, first, core, qa, qb, keys, values):
    picks = ids.shape[1]
    rows, width = 2 * qa.shape[0], qa.shape[1]
    blocks = rows // BLK
    span, wide = picks * BLK, BLK * (width // HD)
    work = rows * width * span
    kept = [((blocks, KEPT_ROWS, wide), jnp.float32), ((blocks, wide, HD), qa.dtype)]
    return pl.pallas_call(
        functools.partial(near_kernel, first),
        out_shape=[jax.ShapeDtypeStruct(*what) for what in kept],
        in_specs=[SMEM, SMEM, VMEM, VMEM, HBM, HBM],
        out_specs=[HBM] * 2,
        scratch_shapes=[
            pltpu.VMEM((rows, width), qa.dtype),
            pltpu.VMEM((blocks, span, HD), keys.dtype),
            pltpu.VMEM((blocks, span, HD), keys.dtype),
            *[pltpu.VMEM(*what) for what in kept],
            pltpu.SemaphoreType.DMA((blocks,)),
            pltpu.SemaphoreType.DMA((blocks,)),
            pltpu.SemaphoreType.DMA((2,)),
        ],
        cost_estimate=cost(4 * work, 8 * rows * width + 4 * blocks * span * HD, work // HD),
    )(ids, core, qa, qb, keys, values)


def far_kernel(firsts, slots_ref, core_ref, got_ref, *refs):
    groups = len(firsts)
    near_refs, o_refs = refs[: 2 * groups], refs[2 * groups : 3 * groups]
    far_buf, o_buf, far_sem = refs[3 * groups :]
    picks, half = far_buf.shape[1], o_buf.shape[2]
    ratio, blocks = o_buf.shape[3] // HD, far_buf.shape[0] // groups
    factor = HD ** (-0.5) * LOG2E
    core = core_ref[0]
    for n in range(groups * blocks):
        g, i = divmod(n, blocks)
        for j in range(picks):
            pltpu.make_async_copy(got_ref.at[slots_ref[firsts[g] + i, j]], far_buf.at[n, j], far_sem).start()
    wait_for(far_buf, far_sem)
    for n in range(groups * blocks):
        g, i = divmod(n, blocks)
        kept_ref, q_ref = near_refs[2 * g : 2 * g + 2]
        keys = jnp.concatenate([far_buf[n, j, 0] for j in range(picks)], axis=0)
        values = jnp.concatenate([far_buf[n, j, 1] for j in range(picks)], axis=0)
        for r in range(ratio):
            queries = slice(r * BLK, (r + 1) * BLK)
            score = scores_of(keys, q_ref[i, queries, :])
            before = kept_ref[i, HIGHEST : HIGHEST + 1, queries]
            highest = jnp.maximum(jnp.max(score, axis=0, keepdims=True) * factor, before)
            exponent = jnp.exp2(score * factor - highest)
            kept = jnp.exp2(before - highest)
            total = jnp.sum(exponent, axis=0, keepdims=True) + kept * kept_ref[i, TOTAL : TOTAL + 1, queries]
            partial = weighted(values, exponent.astype(jnp.bfloat16))
            merged = (partial + kept * kept_ref[i, 0:HD, queries]) * (1.0 / total)
            turned = merged.T.astype(o_buf.dtype)
            for part in range(CORES):
                low, high = max(i * BLK, part * half), min((i + 1) * BLK, (part + 1) * half)
                if low < high:
                    rows = slice(low - part * half, high - part * half)
                    o_buf[g, part, rows, r * HD : (r + 1) * HD] = turned[low - i * BLK : high - i * BLK]
    for g in range(groups):
        for part in range(CORES):
            o_refs[g][core if part == 0 else 1 - core] = o_buf[g, part]


def far_attention(slots, firsts, core, got, near):
    groups, picks = len(firsts), slots.shape[1]
    _, q = near[0]
    blocks, wide = q.shape[0], q.shape[1]
    count = groups * blocks
    half, width = blocks * BLK // CORES, wide // BLK * HD
    return pl.pallas_call(
        functools.partial(far_kernel, firsts),
        out_shape=[jax.ShapeDtypeStruct((CORES, half, width), q.dtype)] * groups,
        in_specs=[SMEM, SMEM, HBM] + [VMEM] * (2 * groups),
        out_specs=[VMEM] * groups,
        scratch_shapes=[
            pltpu.VMEM((count, picks) + got.shape[1:], got.dtype),
            pltpu.VMEM((groups, CORES, half, width), q.dtype),
            pltpu.SemaphoreType.DMA,
        ],
        compiler_params=room(16),
        cost_estimate=cost(1, 1),
    )(slots, core, got, *[array for group in near for array in group])


def offset_pairs(chips, chip_step, core_step):
    return [
        (chip * CORES + core, (chip + chip_step) % chips * CORES + (core ^ core_step))
        for chip in range(chips)
        for core in range(CORES)
    ]


def shards(queries, cache_keys, cache_values, block_ids):
    seq_count = lax.axis_size("seq")
    heads = lax.axis_size("head")
    seq_place = lax.axis_index("seq")
    head_place = lax.axis_index("head")
    chips = heads // CORES
    chip, core = head_place // CORES, head_place % CORES
    q_count, k_count = block_ids.shape[0], cache_keys.shape[0] // BLK
    per_chip = q_count // chips
    far_count = block_ids.shape[1] - NEAR
    capacity = max(2, (far_count * q_count + seq_count - 2) // (seq_count - 1))
    slot_total = seq_count * capacity

    far_ids = block_ids[:, NEAR:].reshape(-1)
    far_owner = far_ids // k_count
    far_within = far_ids - far_owner * k_count
    entry = jnp.arange(far_ids.shape[0], dtype=jnp.int32)
    earlier = (far_owner[:, None] == far_owner[None, :]) & (entry[None, :] < entry[:, None])
    far_slot = far_owner * capacity + jnp.sum(earlier.astype(jnp.int32), axis=1)
    slot_range = jnp.arange(slot_total, dtype=jnp.int32)
    unasked = slot_range % k_count
    placed = far_slot[:, None] == slot_range[None, :]
    asked = unasked + jnp.sum(jnp.where(placed, far_within[:, None] - unasked[None, :], 0), axis=0)
    wanted = lax.all_to_all(asked.reshape(seq_count, 1, capacity), "seq", split_axis=0, concat_axis=0, tiled=True)

    sent = pack(wanted, hold(cache_keys), cache_values)
    got = lax.all_to_all(
        sent.reshape(seq_count, capacity, 2, BLK, HD), "seq", split_axis=0, concat_axis=0, tiled=True
    ).reshape(slot_total, 2, BLK, HD)

    steps = [(d, e) for d in range(chips) for e in range(CORES)]
    step_chip = jnp.array([d for d, _ in steps], jnp.int32)
    step_core = jnp.array([e for _, e in steps], jnp.int32)
    ahead = (chip + step_chip) % chips * CORES + (core + step_core) % CORES
    pieces = split_queries(queries, ahead)
    rows_of = {}
    for piece, (d, e) in zip(pieces, steps):
        rows_of[d, e] = piece if d == e == 0 else lax.ppermute(piece, "head", offset_pairs(chips, d, e))

    order = (chip - jnp.arange(chips, dtype=jnp.int32)) % chips
    own_ids = jnp.concatenate([block_ids[:, :NEAR] - seq_place * k_count, far_slot.reshape(q_count, far_count)], axis=1)
    own_ids = jnp.take(own_ids.reshape(chips, per_chip, -1), order, axis=0).reshape(q_count, -1)
    near_ids, slots = own_ids[:, :NEAR], own_ids[:, NEAR:]
    core_operand = core.astype(jnp.int32).reshape(1)
    near = [
        near_attention(near_ids, d * per_chip, core_operand, rows_of[d, 0], rows_of[d, 1], cache_keys, cache_values)
        for d in range(chips)
    ]
    got, near, slots = lax.optimization_barrier((got, near, slots))

    results = [None] * chips
    distance = lambda d: min(d, chips - d)
    for hops in range(chips // 2, -1, -1):
        group = [d for d in range(chips) if distance(d) == hops]
        if not hops:
            got, results[chips // 2] = lax.optimization_barrier((got, results[chips // 2]))
        made = far_attention(slots, tuple(d * per_chip for d in group), core_operand, got, [near[d] for d in group])
        if hops:
            made, got = lax.optimization_barrier((made, got))
        for d, rows in zip(group, made):
            results[d] = lax.ppermute(rows, "head", offset_pairs(chips, -d, 0)) if d else rows
    joined = []
    for d in range(chips):
        joined += [results[d], lax.ppermute(results[d], "head", offset_pairs(chips, 0, 1))]
    early = tuple(i for i in range(heads) if i // CORES in (0, chips // 2))
    late = tuple(i for i in range(heads) if i not in early)
    return join_outputs(joined, late, ahead, join_outputs(joined, early, ahead))


def solution(mesh):
    return jax.shard_map(
        shards,
        mesh=mesh,
        in_specs=(P(("seq", "head"), None), P("seq", "head"), P("seq", "head"), P("seq", None)),
        out_specs=P(("seq", "head"), None),
        check_vma=False,
    )
```

```python
import functools

import jax
import jax.numpy as jnp
from jax import lax
from jax.experimental import pallas as pl
from jax.experimental.pallas import tpu as pltpu
from jax.sharding import PartitionSpec as P

HD = 128
BLK = 128
NEAR = 5
CORES = 2
HBM = pl.BlockSpec(memory_space=pltpu.HBM)
SMEM = pl.BlockSpec(memory_space=pltpu.SMEM)
VMEM = pl.BlockSpec(memory_space=pltpu.VMEM)
LOG2E = 1.4426950408889634
HIGHEST, TOTAL, KEPT_ROWS = HD, HD + 1, HD + 8


def wait_for(ref, sem):
    pltpu.make_async_copy(ref, ref, sem).wait()


def room(mebibytes):
    return pltpu.CompilerParams(vmem_limit_bytes=mebibytes * 1024 * 1024)


def cost(flops, bytes_accessed, transcendentals=0):
    return pl.CostEstimate(flops=flops, bytes_accessed=bytes_accessed, transcendentals=transcendentals)


def split_queries_kernel(places_ref, q_ref, *refs):
    count = len(refs) - 3
    outs, buf, in_sem, out_sem = refs[:count], *refs[count:]
    width = buf.shape[2]
    into, out_of = [], []
    for i in range(count):
        start = pl.multiple_of(places_ref[i] * width, width)
        into.append(pltpu.make_async_copy(q_ref.at[:, pl.ds(start, width)], buf.at[i], in_sem.at[i]))
        out_of.append(pltpu.make_async_copy(buf.at[i], outs[i], out_sem.at[i]))
    for copy in into:
        copy.start()
    for i in range(count):
        into[i].wait()
        out_of[i].start()
    for copy in out_of:
        copy.wait()


def split_queries(queries, places):
    count = places.shape[0]
    rows, width = queries.shape[0], queries.shape[1] // count
    return pl.pallas_call(
        split_queries_kernel,
        out_shape=[jax.ShapeDtypeStruct((rows, width), queries.dtype)] * count,
        in_specs=[SMEM, HBM],
        out_specs=[HBM] * count,
        scratch_shapes=[
            pltpu.VMEM((count, rows, width), queries.dtype),
            pltpu.SemaphoreType.DMA((count,)),
            pltpu.SemaphoreType.DMA((count,)),
        ],
        cost_estimate=cost(0, 4 * queries.size),
    )(places, queries)


def join_outputs_kernel(count, chosen, places_ref, *refs):
    pieces, out_ref, sem = refs[: len(chosen)], refs[-2], refs[-1]
    width = out_ref.shape[1] // count
    copies = []
    for piece, i in zip(pieces, chosen):
        start = pl.multiple_of(places_ref[i] * width, width)
        copies.append(pltpu.make_async_copy(piece.at[i % CORES], out_ref.at[:, pl.ds(start, width)], sem.at[i]))
    for copy in copies:
        copy.start()
    for copy in copies:
        copy.wait()


def join_outputs(pieces, chosen, places, out=None):
    count = len(pieces)
    _, rows, width = pieces[0].shape
    rest = [] if out is None else [out]
    return pl.pallas_call(
        functools.partial(join_outputs_kernel, count, chosen),
        out_shape=jax.ShapeDtypeStruct((rows, width * count), pieces[0].dtype),
        in_specs=[SMEM] + [VMEM] * len(chosen) + [HBM] * len(rest),
        out_specs=HBM,
        scratch_shapes=[pltpu.SemaphoreType.DMA((count,))],
        input_output_aliases={1 + len(chosen): 0} if rest else {},
        compiler_params=room(6),
        cost_estimate=cost(0, 4 * rows * width * len(chosen)),
    )(places, *[pieces[i] for i in chosen], *rest)


def hold_kernel(k_ref, k_out, sem):
    copy = pltpu.make_async_copy(k_ref, k_out, sem)
    copy.start()
    copy.wait()


def hold(keys):
    return pl.pallas_call(
        hold_kernel,
        out_shape=jax.ShapeDtypeStruct(keys.shape, keys.dtype),
        in_specs=[HBM],
        out_specs=VMEM,
        scratch_shapes=[pltpu.SemaphoreType.DMA],
        compiler_params=room(6),
        cost_estimate=cost(0, 4 * keys.size),
    )(keys)


def pack_kernel(wanted_ref, k_ref, v_ref, out_ref):
    capacity = wanted_ref.shape[2]
    for place in range(out_ref.shape[0]):
        wanted = wanted_ref[place // capacity, 0, place % capacity]
        rows = pl.ds(pl.multiple_of(wanted * BLK, BLK), BLK)
        out_ref[place, 0] = k_ref[rows, :]
        out_ref[place, 1] = v_ref[rows, :]


def pack(wanted, keys, values):
    count = wanted.shape[0] * wanted.shape[2]
    return pl.pallas_call(
        pack_kernel,
        out_shape=jax.ShapeDtypeStruct((count, 2, BLK, HD), keys.dtype),
        in_specs=[SMEM, VMEM, VMEM],
        out_specs=VMEM,
        compiler_params=room(12),
        cost_estimate=cost(0, 8 * count * BLK * HD),
    )(wanted, keys, values)


def scores_of(keys, queries):
    return lax.dot_general(keys, queries, (((1,), (1,)), ((), ())), preferred_element_type=jnp.float32)


def weighted(values, weights):
    return lax.dot_general(values, weights, (((0,), (0,)), ((), ())), preferred_element_type=jnp.float32)


def near_kernel(first, ids_ref, core_ref, qa_ref, qb_ref, k_ref, v_ref, kept_out, q_out, q_buf, k_buf, v_buf, kept_ref, q_ref, k_sem, v_sem, out_sem):
    blocks, picks, half = q_ref.shape[0], k_buf.shape[1] // BLK, qa_ref.shape[0]
    ratio = q_buf.shape[1] // HD
    factor = HD ** (-0.5) * LOG2E
    core = core_ref[0]
    for i in range(blocks):
        for j in range(picks):
            held = pl.ds(pl.multiple_of(ids_ref[first + i, j] * BLK, BLK), BLK)
            pltpu.make_async_copy(k_ref.at[held], k_buf.at[i, pl.ds(j * BLK, BLK)], k_sem.at[i]).start()
            pltpu.make_async_copy(v_ref.at[held], v_buf.at[i, pl.ds(j * BLK, BLK)], v_sem.at[i]).start()
    q_buf[pl.ds(pl.multiple_of(core * half, half), half), :] = qa_ref[...]
    q_buf[pl.ds(pl.multiple_of((1 - core) * half, half), half), :] = qb_ref[...]
    for i in range(blocks):
        for r in range(ratio):
            q_ref[i, r * BLK : (r + 1) * BLK, :] = q_buf[i * BLK : (i + 1) * BLK, r * HD : (r + 1) * HD]
    q_copy = pltpu.make_async_copy(q_ref, q_out, out_sem.at[0])
    q_copy.start()

    def block(i, carry):
        wait_for(k_buf.at[i], k_sem.at[i])
        wait_for(v_buf.at[i], v_sem.at[i])
        score = scores_of(k_buf[i], q_ref[i])
        highest = jnp.max(score, axis=0, keepdims=True) * factor
        exponent = jnp.exp2(score * factor - highest)
        kept_ref[i, HIGHEST : HIGHEST + 1, :] = highest
        kept_ref[i, TOTAL : TOTAL + 1, :] = jnp.sum(exponent, axis=0, keepdims=True)
        kept_ref[i, 0:HD, :] = weighted(v_buf[i], exponent.astype(jnp.bfloat16))
        return carry

    lax.fori_loop(0, blocks, block, 0)
    kept_copy = pltpu.make_async_copy(kept_ref, kept_out, out_sem.at[1])
    kept_copy.start()
    q_copy.wait()
    kept_copy.wait()


def near_attention(ids, first, core, qa, qb, keys, values):
    picks = ids.shape[1]
    rows, width = 2 * qa.shape[0], qa.shape[1]
    blocks = rows // BLK
    span, wide = picks * BLK, BLK * (width // HD)
    work = rows * width * span
    kept = [((blocks, KEPT_ROWS, wide), jnp.float32), ((blocks, wide, HD), qa.dtype)]
    return pl.pallas_call(
        functools.partial(near_kernel, first),
        out_shape=[jax.ShapeDtypeStruct(*what) for what in kept],
        in_specs=[SMEM, SMEM, VMEM, VMEM, HBM, HBM],
        out_specs=[HBM] * 2,
        scratch_shapes=[
            pltpu.VMEM((rows, width), qa.dtype),
            pltpu.VMEM((blocks, span, HD), keys.dtype),
            pltpu.VMEM((blocks, span, HD), keys.dtype),
            *[pltpu.VMEM(*what) for what in kept],
            pltpu.SemaphoreType.DMA((blocks,)),
            pltpu.SemaphoreType.DMA((blocks,)),
            pltpu.SemaphoreType.DMA((2,)),
        ],
        cost_estimate=cost(4 * work, 8 * rows * width + 4 * blocks * span * HD, work // HD),
    )(ids, core, qa, qb, keys, values)


def far_kernel(firsts, slots_ref, core_ref, got_ref, *refs):
    groups = len(firsts)
    near_refs, o_refs = refs[: 2 * groups], refs[2 * groups : 3 * groups]
    far_buf, o_buf, far_sem = refs[3 * groups :]
    picks, half = far_buf.shape[1], o_buf.shape[2]
    ratio, blocks = o_buf.shape[3] // HD, far_buf.shape[0] // groups
    factor = HD ** (-0.5) * LOG2E
    core = core_ref[0]
    for n in range(groups * blocks):
        g, i = divmod(n, blocks)
        for j in range(picks):
            pltpu.make_async_copy(got_ref.at[slots_ref[firsts[g] + i, j]], far_buf.at[n, j], far_sem).start()
    wait_for(far_buf, far_sem)
    for n in range(groups * blocks):
        g, i = divmod(n, blocks)
        kept_ref, q_ref = near_refs[2 * g : 2 * g + 2]
        keys = jnp.concatenate([far_buf[n, j, 0] for j in range(picks)], axis=0)
        values = jnp.concatenate([far_buf[n, j, 1] for j in range(picks)], axis=0)
        for r in range(ratio):
            queries = slice(r * BLK, (r + 1) * BLK)
            score = scores_of(keys, q_ref[i, queries, :])
            before = kept_ref[i, HIGHEST : HIGHEST + 1, queries]
            highest = jnp.maximum(jnp.max(score, axis=0, keepdims=True) * factor, before)
            exponent = jnp.exp2(score * factor - highest)
            kept = jnp.exp2(before - highest)
            total = jnp.sum(exponent, axis=0, keepdims=True) + kept * kept_ref[i, TOTAL : TOTAL + 1, queries]
            partial = weighted(values, exponent.astype(jnp.bfloat16))
            merged = (partial + kept * kept_ref[i, 0:HD, queries]) * (1.0 / total)
            turned = merged.T.astype(o_buf.dtype)
            for part in range(CORES):
                low, high = max(i * BLK, part * half), min((i + 1) * BLK, (part + 1) * half)
                if low < high:
                    rows = slice(low - part * half, high - part * half)
                    o_buf[g, part, rows, r * HD : (r + 1) * HD] = turned[low - i * BLK : high - i * BLK]
    for g in range(groups):
        for part in range(CORES):
            o_refs[g][core if part == 0 else 1 - core] = o_buf[g, part]


def far_attention(slots, firsts, core, got, near):
    groups, picks = len(firsts), slots.shape[1]
    _, q = near[0]
    blocks, wide = q.shape[0], q.shape[1]
    count = groups * blocks
    half, width = blocks * BLK // CORES, wide // BLK * HD
    return pl.pallas_call(
        functools.partial(far_kernel, firsts),
        out_shape=[jax.ShapeDtypeStruct((CORES, half, width), q.dtype)] * groups,
        in_specs=[SMEM, SMEM, HBM] + [VMEM] * (2 * groups),
        out_specs=[VMEM] * groups,
        scratch_shapes=[
            pltpu.VMEM((count, picks) + got.shape[1:], got.dtype),
            pltpu.VMEM((groups, CORES, half, width), q.dtype),
            pltpu.SemaphoreType.DMA,
        ],
        compiler_params=room(16),
        cost_estimate=cost(1, 1),
    )(slots, core, got, *[array for group in near for array in group])


def offset_pairs(chips, chip_step, core_step):
    return [
        (chip * CORES + core, (chip + chip_step) % chips * CORES + (core ^ core_step))
        for chip in range(chips)
        for core in range(CORES)
    ]


def shards(queries, cache_keys, cache_values, block_ids):
    seq_count = lax.axis_size("seq")
    heads = lax.axis_size("head")
    seq_place = lax.axis_index("seq")
    head_place = lax.axis_index("head")
    chips = heads // CORES
    chip, core = head_place // CORES, head_place % CORES
    q_count, k_count = block_ids.shape[0], cache_keys.shape[0] // BLK
    per_chip = q_count // chips
    far_count = block_ids.shape[1] - NEAR
    capacity = max(2, (far_count * q_count + seq_count - 2) // (seq_count - 1))
    slot_total = seq_count * capacity

    far_ids = block_ids.T[NEAR:]
    far_owner = far_ids // k_count
    far_within = far_ids - far_owner * k_count
    entry = lax.broadcasted_iota(jnp.int32, far_ids.shape, 1) * far_count + lax.broadcasted_iota(jnp.int32, far_ids.shape, 0)
    earlier = (far_owner[:, :, None, None] == far_owner[None, None]) & (entry[None, None] < entry[:, :, None, None])
    far_slot = far_owner * capacity + jnp.sum(earlier.astype(jnp.int32), axis=(2, 3))
    slot_range = jnp.arange(slot_total, dtype=jnp.int32)
    unasked = slot_range % k_count
    placed = far_slot[:, :, None] == slot_range
    asked = unasked + jnp.sum(jnp.where(placed, far_within[:, :, None] - unasked, 0), axis=(0, 1))
    wanted = lax.all_to_all(asked.reshape(seq_count, 1, capacity), "seq", split_axis=0, concat_axis=0, tiled=True)

    sent = pack(wanted, hold(cache_keys), cache_values)
    got = lax.all_to_all(
        sent.reshape(seq_count, capacity, 2, BLK, HD), "seq", split_axis=0, concat_axis=0, tiled=True
    ).reshape(slot_total, 2, BLK, HD)

    steps = [(d, e) for d in range(chips) for e in range(CORES)]
    step_chip = jnp.array([d for d, _ in steps], jnp.int32)
    step_core = jnp.array([e for _, e in steps], jnp.int32)
    ahead = (chip + step_chip) % chips * CORES + (core + step_core) % CORES
    pieces = split_queries(queries, ahead)
    rows_of = {}
    for piece, (d, e) in zip(pieces, steps):
        rows_of[d, e] = piece if d == e == 0 else lax.ppermute(piece, "head", offset_pairs(chips, d, e))

    order = (chip - jnp.arange(chips, dtype=jnp.int32)) % chips
    own_ids = jnp.concatenate([block_ids[:, :NEAR] - seq_place * k_count, far_slot.T], axis=1)
    own_ids = jnp.take(own_ids.reshape(chips, per_chip, -1), order, axis=0).reshape(q_count, -1)
    near_ids, slots = own_ids[:, :NEAR], own_ids[:, NEAR:]
    core_operand = core.astype(jnp.int32).reshape(1)
    near = [
        near_attention(near_ids, d * per_chip, core_operand, rows_of[d, 0], rows_of[d, 1], cache_keys, cache_values)
        for d in range(chips)
    ]
    got, near, slots = lax.optimization_barrier((got, near, slots))

    results = [None] * chips
    distance = lambda d: min(d, chips - d)
    for hops in range(chips // 2, -1, -1):
        group = [d for d in range(chips) if distance(d) == hops]
        if not hops:
            got, results[chips // 2] = lax.optimization_barrier((got, results[chips // 2]))
        made = far_attention(slots, tuple(d * per_chip for d in group), core_operand, got, [near[d] for d in group])
        if hops:
            made, got = lax.optimization_barrier((made, got))
        for d, rows in zip(group, made):
            results[d] = lax.ppermute(rows, "head", offset_pairs(chips, -d, 0)) if d else rows
    joined = []
    for d in range(chips):
        joined += [results[d], lax.ppermute(results[d], "head", offset_pairs(chips, 0, 1))]
    early = tuple(i for i in range(heads) if i // CORES in (0, chips // 2))
    late = tuple(i for i in range(heads) if i not in early)
    return join_outputs(joined, late, ahead, join_outputs(joined, early, ahead))


def solution(mesh):
    return jax.shard_map(
        shards,
        mesh=mesh,
        in_specs=(P(("seq", "head"), None), P("seq", "head"), P("seq", "head"), P("seq", None)),
        out_specs=P(("seq", "head"), None),
        check_vma=False,
    )
```

```python
import functools

import jax
import jax.numpy as jnp
from jax import lax
from jax.experimental import pallas as pl
from jax.experimental.pallas import tpu as pltpu
from jax.sharding import PartitionSpec as P

HD = 128
BLK = 128
NEAR = 5
CORES = 2
HBM = pl.BlockSpec(memory_space=pltpu.HBM)
SMEM = pl.BlockSpec(memory_space=pltpu.SMEM)
VMEM = pl.BlockSpec(memory_space=pltpu.VMEM)
LOG2E = 1.4426950408889634
HIGHEST, TOTAL, KEPT_ROWS = HD, HD + 1, HD + 8


def wait_for(ref, sem):
    pltpu.make_async_copy(ref, ref, sem).wait()


def room(mebibytes):
    return pltpu.CompilerParams(vmem_limit_bytes=mebibytes * 1024 * 1024)


def cost(flops, bytes_accessed, transcendentals=0):
    return pl.CostEstimate(flops=flops, bytes_accessed=bytes_accessed, transcendentals=transcendentals)


def split_queries_kernel(places_ref, q_ref, *refs):
    count = len(refs) - 3
    outs, buf, in_sem, out_sem = refs[:count], *refs[count:]
    width = buf.shape[2]
    into, out_of = [], []
    for i in range(count):
        start = pl.multiple_of(places_ref[i] * width, width)
        into.append(pltpu.make_async_copy(q_ref.at[:, pl.ds(start, width)], buf.at[i], in_sem.at[i]))
        out_of.append(pltpu.make_async_copy(buf.at[i], outs[i], out_sem.at[i]))
    for copy in into:
        copy.start()
    for i in range(count):
        into[i].wait()
        out_of[i].start()
    for copy in out_of:
        copy.wait()


def split_queries(queries, places):
    count = places.shape[0]
    rows, width = queries.shape[0], queries.shape[1] // count
    return pl.pallas_call(
        split_queries_kernel,
        out_shape=[jax.ShapeDtypeStruct((rows, width), queries.dtype)] * count,
        in_specs=[SMEM, HBM],
        out_specs=[HBM] * count,
        scratch_shapes=[
            pltpu.VMEM((count, rows, width), queries.dtype),
            pltpu.SemaphoreType.DMA((count,)),
            pltpu.SemaphoreType.DMA((count,)),
        ],
        cost_estimate=cost(0, 4 * queries.size),
    )(places, queries)


def join_outputs_kernel(count, chosen, places_ref, *refs):
    pieces, out_ref, sem = refs[: len(chosen)], refs[-2], refs[-1]
    width = out_ref.shape[1] // count
    copies = []
    for piece, i in zip(pieces, chosen):
        start = pl.multiple_of(places_ref[i] * width, width)
        copies.append(pltpu.make_async_copy(piece.at[i % CORES], out_ref.at[:, pl.ds(start, width)], sem.at[i]))
    for copy in copies:
        copy.start()
    for copy in copies:
        copy.wait()


def join_outputs(pieces, chosen, places, out=None):
    count = len(pieces)
    _, rows, width = pieces[0].shape
    rest = [] if out is None else [out]
    return pl.pallas_call(
        functools.partial(join_outputs_kernel, count, chosen),
        out_shape=jax.ShapeDtypeStruct((rows, width * count), pieces[0].dtype),
        in_specs=[SMEM] + [VMEM] * len(chosen) + [HBM] * len(rest),
        out_specs=HBM,
        scratch_shapes=[pltpu.SemaphoreType.DMA((count,))],
        input_output_aliases={1 + len(chosen): 0} if rest else {},
        compiler_params=room(6),
        cost_estimate=cost(0, 4 * rows * width * len(chosen)),
    )(places, *[pieces[i] for i in chosen], *rest)


def pack_kernel(chunks, unroll, wanted_ref, k_ref, v_ref, out_ref, buf, in_sem, out_sem):
    span, capacity = out_ref.shape[0] // chunks, wanted_ref.shape[2]
    owners = span // capacity
    copies = []
    for chunk in range(chunks):

        def fetch(owner, carry):
            for j in range(capacity):
                rows = pl.ds(pl.multiple_of(wanted_ref[owner, 0, j] * BLK, BLK), BLK)
                place = owner * capacity + j
                pltpu.make_async_copy(k_ref.at[rows], buf.at[place, 0], in_sem.at[chunk]).start()
                pltpu.make_async_copy(v_ref.at[rows], buf.at[place, 1], in_sem.at[chunk]).start()
            return carry

        lax.fori_loop(chunk * owners, (chunk + 1) * owners, fetch, 0, unroll=unroll)
    for chunk in range(chunks):
        part = pl.ds(chunk * span, span)
        wait_for(buf.at[part], in_sem.at[chunk])
        copies.append(pltpu.make_async_copy(buf.at[part], out_ref.at[part], out_sem.at[chunk]))
        copies[-1].start()
    for copy in copies:
        copy.wait()


def pack(wanted, keys, values, chunks=4, unroll=2):
    count = wanted.shape[0] * wanted.shape[2]
    return pl.pallas_call(
        functools.partial(pack_kernel, chunks, unroll),
        out_shape=jax.ShapeDtypeStruct((count, 2, BLK, HD), keys.dtype),
        in_specs=[SMEM, HBM, HBM],
        out_specs=HBM,
        scratch_shapes=[
            pltpu.VMEM((count, 2, BLK, HD), keys.dtype),
            pltpu.SemaphoreType.DMA((chunks,)),
            pltpu.SemaphoreType.DMA((chunks,)),
        ],
        cost_estimate=cost(0, 8 * count * BLK * HD),
    )(wanted, keys, values)


def scores_of(keys, queries):
    return lax.dot_general(keys, queries, (((1,), (1,)), ((), ())), preferred_element_type=jnp.float32)


def weighted(values, weights):
    return lax.dot_general(values, weights, (((0,), (0,)), ((), ())), preferred_element_type=jnp.float32)


def near_kernel(first, ids_ref, core_ref, qa_ref, qb_ref, k_ref, v_ref, kept_out, q_out, q_buf, k_buf, v_buf, kept_ref, q_ref, k_sem, v_sem, out_sem):
    blocks, picks, half = q_ref.shape[0], k_buf.shape[1] // BLK, qa_ref.shape[0]
    ratio = q_buf.shape[1] // HD
    factor = HD ** (-0.5) * LOG2E
    core = core_ref[0]
    for i in range(blocks):
        for j in range(picks):
            held = pl.ds(pl.multiple_of(ids_ref[first + i, j] * BLK, BLK), BLK)
            pltpu.make_async_copy(k_ref.at[held], k_buf.at[i, pl.ds(j * BLK, BLK)], k_sem.at[i]).start()
            pltpu.make_async_copy(v_ref.at[held], v_buf.at[i, pl.ds(j * BLK, BLK)], v_sem.at[i]).start()
    q_buf[pl.ds(pl.multiple_of(core * half, half), half), :] = qa_ref[...]
    q_buf[pl.ds(pl.multiple_of((1 - core) * half, half), half), :] = qb_ref[...]
    for i in range(blocks):
        for r in range(ratio):
            q_ref[i, r * BLK : (r + 1) * BLK, :] = q_buf[i * BLK : (i + 1) * BLK, r * HD : (r + 1) * HD]
    q_copy = pltpu.make_async_copy(q_ref, q_out, out_sem.at[0])
    q_copy.start()

    def block(i, carry):
        wait_for(k_buf.at[i], k_sem.at[i])
        wait_for(v_buf.at[i], v_sem.at[i])
        score = scores_of(k_buf[i], q_ref[i])
        highest = jnp.max(score, axis=0, keepdims=True) * factor
        exponent = jnp.exp2(score * factor - highest)
        kept_ref[i, HIGHEST : HIGHEST + 1, :] = highest
        kept_ref[i, TOTAL : TOTAL + 1, :] = jnp.sum(exponent, axis=0, keepdims=True)
        kept_ref[i, 0:HD, :] = weighted(v_buf[i], exponent.astype(jnp.bfloat16))
        return carry

    lax.fori_loop(0, blocks, block, 0)
    kept_copy = pltpu.make_async_copy(kept_ref, kept_out, out_sem.at[1])
    kept_copy.start()
    q_copy.wait()
    kept_copy.wait()


def near_attention(ids, first, core, qa, qb, keys, values):
    picks = ids.shape[1]
    rows, width = 2 * qa.shape[0], qa.shape[1]
    blocks = rows // BLK
    span, wide = picks * BLK, BLK * (width // HD)
    work = rows * width * span
    kept = [((blocks, KEPT_ROWS, wide), jnp.float32), ((blocks, wide, HD), qa.dtype)]
    return pl.pallas_call(
        functools.partial(near_kernel, first),
        out_shape=[jax.ShapeDtypeStruct(*what) for what in kept],
        in_specs=[SMEM, SMEM, VMEM, VMEM, HBM, HBM],
        out_specs=[HBM] * 2,
        scratch_shapes=[
            pltpu.VMEM((rows, width), qa.dtype),
            pltpu.VMEM((blocks, span, HD), keys.dtype),
            pltpu.VMEM((blocks, span, HD), keys.dtype),
            *[pltpu.VMEM(*what) for what in kept],
            pltpu.SemaphoreType.DMA((blocks,)),
            pltpu.SemaphoreType.DMA((blocks,)),
            pltpu.SemaphoreType.DMA((2,)),
        ],
        cost_estimate=cost(4 * work, 8 * rows * width + 4 * blocks * span * HD, work // HD),
    )(ids, core, qa, qb, keys, values)


def far_kernel(firsts, slots_ref, core_ref, got_ref, *refs):
    groups = len(firsts)
    near_refs, o_refs = refs[: 2 * groups], refs[2 * groups : 3 * groups]
    far_buf, o_buf, far_sem = refs[3 * groups :]
    picks, half = far_buf.shape[1], o_buf.shape[2]
    ratio, blocks = o_buf.shape[3] // HD, far_buf.shape[0] // groups
    factor = HD ** (-0.5) * LOG2E
    core = core_ref[0]
    for n in range(groups * blocks):
        g, i = divmod(n, blocks)
        for j in range(picks):
            pltpu.make_async_copy(got_ref.at[slots_ref[firsts[g] + i, j]], far_buf.at[n, j], far_sem).start()
    wait_for(far_buf, far_sem)
    for n in range(groups * blocks):
        g, i = divmod(n, blocks)
        kept_ref, q_ref = near_refs[2 * g : 2 * g + 2]
        keys = jnp.concatenate([far_buf[n, j, 0] for j in range(picks)], axis=0)
        values = jnp.concatenate([far_buf[n, j, 1] for j in range(picks)], axis=0)
        for r in range(ratio):
            queries = slice(r * BLK, (r + 1) * BLK)
            score = scores_of(keys, q_ref[i, queries, :])
            before = kept_ref[i, HIGHEST : HIGHEST + 1, queries]
            highest = jnp.maximum(jnp.max(score, axis=0, keepdims=True) * factor, before)
            exponent = jnp.exp2(score * factor - highest)
            kept = jnp.exp2(before - highest)
            total = jnp.sum(exponent, axis=0, keepdims=True) + kept * kept_ref[i, TOTAL : TOTAL + 1, queries]
            partial = weighted(values, exponent.astype(jnp.bfloat16))
            merged = (partial + kept * kept_ref[i, 0:HD, queries]) * (1.0 / total)
            turned = merged.T.astype(o_buf.dtype)
            for part in range(CORES):
                low, high = max(i * BLK, part * half), min((i + 1) * BLK, (part + 1) * half)
                if low < high:
                    rows = slice(low - part * half, high - part * half)
                    o_buf[g, part, rows, r * HD : (r + 1) * HD] = turned[low - i * BLK : high - i * BLK]
    for g in range(groups):
        for part in range(CORES):
            o_refs[g][core if part == 0 else 1 - core] = o_buf[g, part]


def far_attention(slots, firsts, core, got, near):
    groups, picks = len(firsts), slots.shape[1]
    _, q = near[0]
    blocks, wide = q.shape[0], q.shape[1]
    count = groups * blocks
    half, width = blocks * BLK // CORES, wide // BLK * HD
    return pl.pallas_call(
        functools.partial(far_kernel, firsts),
        out_shape=[jax.ShapeDtypeStruct((CORES, half, width), q.dtype)] * groups,
        in_specs=[SMEM, SMEM, HBM] + [VMEM] * (2 * groups),
        out_specs=[VMEM] * groups,
        scratch_shapes=[
            pltpu.VMEM((count, picks) + got.shape[1:], got.dtype),
            pltpu.VMEM((groups, CORES, half, width), q.dtype),
            pltpu.SemaphoreType.DMA,
        ],
        compiler_params=room(16),
        cost_estimate=cost(1, 1),
    )(slots, core, got, *[array for group in near for array in group])


def offset_pairs(chips, chip_step, core_step):
    return [
        (chip * CORES + core, (chip + chip_step) % chips * CORES + (core ^ core_step))
        for chip in range(chips)
        for core in range(CORES)
    ]


def shards(queries, cache_keys, cache_values, block_ids):
    seq_count = lax.axis_size("seq")
    heads = lax.axis_size("head")
    seq_place = lax.axis_index("seq")
    head_place = lax.axis_index("head")
    chips = heads // CORES
    chip, core = head_place // CORES, head_place % CORES
    q_count, k_count = block_ids.shape[0], cache_keys.shape[0] // BLK
    per_chip = q_count // chips
    far_count = block_ids.shape[1] - NEAR
    capacity = max(2, (far_count * q_count + seq_count - 2) // (seq_count - 1))
    slot_total = seq_count * capacity

    far_ids = block_ids.T[NEAR:]
    far_owner = far_ids // k_count
    far_within = far_ids - far_owner * k_count
    entry = lax.broadcasted_iota(jnp.int32, far_ids.shape, 1) * far_count + lax.broadcasted_iota(jnp.int32, far_ids.shape, 0)
    earlier = (far_owner[:, :, None, None] == far_owner[None, None]) & (entry[None, None] < entry[:, :, None, None])
    far_slot = far_owner * capacity + jnp.sum(earlier.astype(jnp.int32), axis=(2, 3))
    slot_range = jnp.arange(slot_total, dtype=jnp.int32)
    unasked = slot_range % k_count
    placed = far_slot[:, :, None] == slot_range
    asked = unasked + jnp.sum(jnp.where(placed, far_within[:, :, None] - unasked, 0), axis=(0, 1))
    wanted = lax.all_to_all(asked.reshape(seq_count, 1, capacity), "seq", split_axis=0, concat_axis=0, tiled=True)

    sent = pack(wanted, cache_keys, cache_values)
    got = lax.all_to_all(
        sent.reshape(seq_count, capacity, 2, BLK, HD), "seq", split_axis=0, concat_axis=0, tiled=True
    ).reshape(slot_total, 2, BLK, HD)

    steps = [(d, e) for d in range(chips) for e in range(CORES)]
    step_chip = jnp.array([d for d, _ in steps], jnp.int32)
    step_core = jnp.array([e for _, e in steps], jnp.int32)
    ahead = (chip + step_chip) % chips * CORES + (core + step_core) % CORES
    pieces = split_queries(queries, ahead)
    rows_of = {}
    for piece, (d, e) in zip(pieces, steps):
        rows_of[d, e] = piece if d == e == 0 else lax.ppermute(piece, "head", offset_pairs(chips, d, e))

    order = (chip - jnp.arange(chips, dtype=jnp.int32)) % chips
    own_ids = jnp.concatenate([block_ids[:, :NEAR] - seq_place * k_count, far_slot.T], axis=1)
    own_ids = jnp.take(own_ids.reshape(chips, per_chip, -1), order, axis=0).reshape(q_count, -1)
    near_ids, slots = own_ids[:, :NEAR], own_ids[:, NEAR:]
    core_operand = core.astype(jnp.int32).reshape(1)
    near = [
        near_attention(near_ids, d * per_chip, core_operand, rows_of[d, 0], rows_of[d, 1], cache_keys, cache_values)
        for d in range(chips)
    ]
    got, near, slots = lax.optimization_barrier((got, near, slots))

    results = [None] * chips
    distance = lambda d: min(d, chips - d)
    for hops in range(chips // 2, -1, -1):
        group = [d for d in range(chips) if distance(d) == hops]
        if not hops:
            got, results[chips // 2] = lax.optimization_barrier((got, results[chips // 2]))
        made = far_attention(slots, tuple(d * per_chip for d in group), core_operand, got, [near[d] for d in group])
        if hops:
            made, got = lax.optimization_barrier((made, got))
        for d, rows in zip(group, made):
            results[d] = lax.ppermute(rows, "head", offset_pairs(chips, -d, 0)) if d else rows
    joined = []
    for d in range(chips):
        joined += [results[d], lax.ppermute(results[d], "head", offset_pairs(chips, 0, 1))]
    early = tuple(i for i in range(heads) if i // CORES in (0, chips // 2))
    late = tuple(i for i in range(heads) if i not in early)
    return join_outputs(joined, late, ahead, join_outputs(joined, early, ahead))


def solution(mesh):
    return jax.shard_map(
        shards,
        mesh=mesh,
        in_specs=(P(("seq", "head"), None), P("seq", "head"), P("seq", "head"), P("seq", None)),
        out_specs=P(("seq", "head"), None),
        check_vma=False,
    )
```
